32 devices in a mesh: seq: 8 (over z, x), mp: 4 (over y, core).
Axes of the slice: x: 2, y: 2, z: 4, core: 2. Of those that a mesh axis runs over, the one named last changes fastest.
Arguments:
- branches: bfloat16 [3, 2048, 4096], P(None, 'seq', 'mp'), may hold values from -6 to 6
- short_filter: float32 [3, 4096, 3], P(None, 'mp'), may hold values from -3.5 to 3.5
- long_filter: bfloat16 [2048, 4096], P('seq', 'mp'), may hold values from -0.125 to 0.125
- skip_gain: float32 [4096], P('mp'), may hold values from 0.5 to 1.5
- out_weight: bfloat16 [4096, 8192], P('mp'), may hold values from -0.09375 to 0.09375
Outputs:
- output: bfloat16 [2048, 8192], P('seq', 'mp')
The draws below stay inside these ranges and needn't reach their ends.
All inputs are finite; a program needn't handle non-finite values.
Results may differ from the reference program's by a relative error of at most 0.015.
Values may be sent and summed in bfloat16 or wider, within the bound.
No kernel may reach another device: no remote copies, remote signals or barrier semaphores. Data moves between devices by JAX's collectives and lax.ppermute only.
A program may use at most 128 MiB of HBM per device.

```python
import jax
import jax.numpy as jnp
from jax import lax

D = 8192
CH_DEV = 1024
TAPS = 3
C = 4096
TOKENS = 2048
N_MP = 4


def block_scale(rng, dims, split, smallest, largest):
    gain = 1.0
    for position, shards_of in split:
        steps = jax.random.uniform(jax.random.fold_in(jax.random.fold_in(rng, 6), position), (shards_of,), jnp.float32, smallest / len(split), largest / len(split))
        gain = gain * jnp.repeat(jnp.exp(steps), dims[position] // shards_of).reshape((-1,) + (1,) * (len(dims) - 1 - position))
    return gain


def normal_values(key, shape, spread, most, pieces=(), held_as=jnp.bfloat16):
    gain = block_scale(key, shape, pieces, -0.22, 0.18) if pieces else 1.0
    entries = jax.random.normal(key, shape, jnp.float32) * spread * gain
    return jnp.minimum(jnp.maximum(entries, -most), most).astype(held_as)


def setup_inputs(seed: int = 0) -> dict:
    key_of = jax.random.split(jax.random.key(seed), 6)
    branches = normal_values(key_of[0], (3, TOKENS, C), 1.0, 6.0, ((1, 8), (2, 4)))
    short_filter = normal_values(key_of[1], (3, C, TAPS), TAPS ** -0.5, 3.5, ((1, 4),), jnp.float32)
    long_filter = normal_values(key_of[2], (TOKENS, C), TOKENS ** -0.5, 0.125, ((0, 8), (1, 4)))
    skip_gain = jnp.clip(0.5 + 1.0 * jax.random.uniform(key_of[3], (C,), jnp.float32) ** block_scale(key_of[3], (C,), ((0, 4),), -0.2, 0.2), 0.5, 1.5)
    out_weight = normal_values(key_of[4], (C, D), C ** -0.5, 0.09375, ((0, 4),))
    return {"branches": branches, "short_filter": short_filter, "long_filter": long_filter, "skip_gain": skip_gain, "out_weight": out_weight}


def reference(branches, short_filter, long_filter, skip_gain, out_weight):
    projected = branches.astype(jnp.float32)
    padded = jnp.pad(projected, ((0, 0), (TAPS - 1, 0), (0, 0)))
    smooth = jnp.zeros((3, TOKENS, C), jnp.float32)
    for tap_id in range(TAPS):
        begin = TAPS - 1 - tap_id
        smooth = smooth + short_filter[:, :, tap_id][:, None, :] * padded[:, begin:begin + TOKENS]
    product = (smooth[0] * smooth[2]).astype(jnp.bfloat16)
    product_f = product.astype(jnp.float32)
    filter_f = long_filter.astype(jnp.float32)
    spectrum = jnp.fft.rfft(product_f, n=2 * TOKENS, axis=0) * jnp.fft.rfft(filter_f, n=2 * TOKENS, axis=0)
    convolved = jnp.fft.irfft(spectrum, n=2 * TOKENS, axis=0)[:TOKENS]
    gated = (smooth[1] * (convolved + skip_gain[None, :] * product_f)).astype(jnp.bfloat16)

    def add_block(running, block_id):
        slab = lax.dynamic_slice_in_dim(gated, block_id * CH_DEV, CH_DEV, 1)
        weight = lax.dynamic_slice_in_dim(out_weight, block_id * CH_DEV, CH_DEV, 0)
        partial_value = jnp.dot(slab, weight, preferred_element_type=jnp.float32).astype(jnp.bfloat16)
        partial_value = lax.optimization_barrier(partial_value)
        return running + partial_value.astype(jnp.float32), None

    start_sum = jnp.zeros((TOKENS, D), jnp.float32)
    summed, unused = lax.scan(add_block, start_sum, jnp.arange(N_MP, dtype=jnp.int32))
    return summed.astype(jnp.bfloat16)
```

```python
import math

import jax
import jax.numpy as jnp
import numpy as np
from jax import lax
from jax.experimental import pallas as pl
from jax.experimental.pallas import tpu as pltpu
from jax.sharding import PartitionSpec as P

ROWS = 16
F32 = jnp.float32
BF16 = jnp.bfloat16


def transform_tables(length, radix):
    ids = np.arange(length)
    angle = 2.0 * math.pi * np.mod(np.outer(ids, ids), length) / length
    cosine, sine = np.cos(angle), np.sin(angle)
    matrix = np.block([[cosine, sine], [-sine, cosine]]).astype(jnp.bfloat16)
    full = length * radix
    turn = 2.0 * math.pi * np.outer(ids, np.arange(1, radix // 2 + 1)) / full
    scale = np.where(np.arange(1, radix // 2 + 1) == radix // 2, 1.0, 2.0) / full
    columns = [np.cos(turn), np.sin(turn), np.cos(turn) * scale, np.sin(turn) * scale]
    return matrix, np.concatenate(columns, axis=1).astype(np.float32)


def axpy(total, factor, value):
    if abs(factor) < 1e-9:
        return total
    if abs(factor - 1.0) < 1e-9:
        return value if total is None else total + value
    if abs(factor + 1.0) < 1e-9:
        return -value if total is None else total - value
    term = value * np.float32(factor)
    return term if total is None else total + term


def wave(step, radix):
    angle = 2.0 * math.pi * (step % radix) / radix
    return math.cos(angle), math.sin(angle)


def across_blocks(values):
    count = len(values)
    radix, half = 2 * count, count // 2
    sums = {n: values[n] + values[count - n] for n in range(1, half)}
    diffs = {n: values[n] - values[count - n] for n in range(1, half)}
    result = []
    for k in range(count + 1):
        in_cos, in_sin = (sums, diffs) if k % 2 == 0 else (diffs, sums)
        real = axpy(values[0], wave(half * k, radix)[0], values[half])
        imag = axpy(None, -wave(half * k, radix)[1], values[half])
        for n in range(1, half):
            cosine, sine = wave(n * k, radix)
            real = axpy(real, cosine, in_cos[n])
            imag = axpy(imag, -sine, in_sin[n])
        result.append((real, imag))
    return result


def back_to_blocks(first, parts):
    count = len(parts)
    radix, half = 2 * count, count // 2
    result = [None] * count
    for n in range(half + 1):
        even_cos, even_sin, odd_cos, odd_sin = first, None, None, None
        for k in range(1, count + 1):
            real, imag = parts[k - 1]
            cosine, sine = wave(n * k, radix)
            if k % 2 == 0:
                even_cos = axpy(even_cos, cosine, real)
                if imag is not None:
                    even_sin = axpy(even_sin, -sine, imag)
            else:
                odd_cos = axpy(odd_cos, cosine, real)
                odd_sin = axpy(odd_sin, -sine, imag)

        def combined(terms):
            total = None
            for sign, term in terms:
                if term is not None:
                    total = axpy(total, sign, term)
            return total

        result[n] = combined([(1, even_cos), (1, even_sin), (1, odd_cos), (1, odd_sin)])
        if 0 < n < half:
            result[count - n] = combined(
                [(1, even_cos), (-1, even_sin), (-1, odd_cos), (1, odd_sin)]
            )
    return result


def convolve_kernel(matrix, twist, gain, signals, out, waves, turned):
    blocks, length, width = out.shape
    pairs = blocks // 2

    def chunk_of(index):
        return pl.ds(pl.multiple_of(index * ROWS, ROWS), ROWS)

    def column(rows, index):
        return jnp.broadcast_to(twist[rows, index : index + 1], (ROWS, width))

    def forward(index, carry):
        rows = chunk_of(index)
        low = pl.ds(pl.multiple_of(length + index * ROWS, ROWS), ROWS)
        for side, source in enumerate((rows, low)):
            lanes = slice(side * width, (side + 1) * width)
            spectra = across_blocks([signals[b, source, :].astype(F32) for b in range(blocks)])
            waves[0, rows, lanes] = spectra[0][0].astype(BF16)
            for k in range(1, blocks + 1):
                real, imag = spectra[k]
                cosine, sine = column(rows, k - 1), column(rows, blocks + k - 1)
                if imag is None:
                    waves[k, rows, lanes] = (real * cosine).astype(BF16)
                    waves[k, low, lanes] = (-real * sine).astype(BF16)
                else:
                    waves[k, rows, lanes] = (real * cosine + imag * sine).astype(BF16)
                    waves[k, low, lanes] = (imag * cosine - real * sine).astype(BF16)
        return carry

    lax.fori_loop(0, length // ROWS, forward, 0)

    def multiplied(spectrum):
        real, imag = spectrum[:length], spectrum[length:]
        a_real, a_imag = real[:, :width], imag[:, :width]
        b_real, b_imag = real[:, width:], imag[:, width:]
        return jnp.concatenate(
            [
                (a_real * b_real - a_imag * b_imag).astype(BF16),
                (-(a_real * b_imag + a_imag * b_real)).astype(BF16),
            ],
            axis=0,
        )

    def dot(left, right):
        return jnp.dot(left, right, preferred_element_type=F32)

    base = multiplied(dot(matrix[:, :length], waves[0, :length, :]))
    turned[pairs, :length, :width] = dot(matrix[:length, :], base)

    def one_pair(pair):
        left = multiplied(dot(matrix[...], waves[2 * pair + 1]))
        right = multiplied(dot(matrix[...], waves[2 * pair + 2]))
        turned[pair] = dot(matrix[...], jnp.concatenate([left, right], axis=1))

    if pairs <= 4:
        for pair in range(pairs):
            one_pair(pair)
    else:
        lax.fori_loop(0, pairs, lambda pair, carry: (one_pair(pair), carry)[1], 0)

    full = 2 * blocks * length
    skip = jnp.broadcast_to(gain[...], (ROWS, width))

    def backward(index, carry):
        rows = chunk_of(index)
        low = pl.ds(pl.multiple_of(length + index * ROWS, ROWS), ROWS)
        parts = []
        for k in range(1, blocks + 1):
            pair, side = (k - 1) // 2, (k - 1) % 2
            lanes = slice(side * width, (side + 1) * width)
            real, minus = turned[pair, rows, lanes], turned[pair, low, lanes]
            cosine, sine = column(rows, 2 * blocks + k - 1), column(rows, 3 * blocks + k - 1)
            turned_real = real * cosine + minus * sine
            parts.append((turned_real, None if k == blocks else real * sine - minus * cosine))
        first = turned[pairs, rows, :width] * np.float32(1.0 / full)
        for b, value in enumerate(back_to_blocks(first, parts)):
            direct = skip * signals[b, rows, :].astype(F32)
            out[b, rows, :] = (value + direct).astype(BF16)
        return carry

    lax.fori_loop(0, length // ROWS, backward, 0)


def convolve(signals, gain):
    blocks, rows, width = signals.shape
    length = rows // 2
    matrix, twist = transform_tables(length, 2 * blocks)
    return pl.pallas_call(
        convolve_kernel,
        out_shape=jax.ShapeDtypeStruct((blocks, length, width), BF16),
        scratch_shapes=[
            pltpu.VMEM((blocks + 1, 2 * length, 2 * width), BF16),
            pltpu.VMEM((blocks // 2 + 1, 2 * length, 2 * width), F32),
        ],
        compiler_params=pltpu.CompilerParams(vmem_limit_bytes=24 << 20),
        name="convolve",
    )(jnp.asarray(matrix), jnp.asarray(twist), gain, signals)


VMEM = pl.BlockSpec(memory_space=pltpu.VMEM)
SMEM = pl.BlockSpec(memory_space=pltpu.SMEM)
HBM = pl.BlockSpec(memory_space=pltpu.HBM)
STRIP = 64
TILE = 512


def smoothed(block, edge, taps, lanes, padded):
    rows, tap_count = block.shape[0], taps.shape[0]
    padded[8 - edge.shape[0] : 8, :] = edge[:, lanes].astype(F32)
    for start in range(0, rows, STRIP):
        padded[8 + start : 8 + start + STRIP, :] = block[start : start + STRIP, lanes].astype(F32)
    for start in range(0, rows, STRIP):
        total = None
        for tap in range(tap_count):
            begin = 8 - tap + start
            term = padded[begin : begin + STRIP, :] * taps[tap : tap + 1, lanes]
            total = term if total is None else total + term
        yield slice(start, start + STRIP), total


def product_kernel(branches, edges, taps, filt, out, padded):
    parts, rows, width = out.shape[0], filt.shape[0], out.shape[2]
    for j in range(parts):
        lanes = slice(j * width, (j + 1) * width)
        first, third = (
            smoothed(branches.at[b], edges.at[b], taps.at[b], lanes, padded.at[j % 2, b // 2])
            for b in (0, 2)
        )
        for (span, left), (span, right) in zip(first, third):
            out[j, span, :] = (left * right).astype(BF16)
        out[j, rows:, :] = filt[:, lanes]


def product_and_filter(branches, edges, taps, filt, parts):
    rows, channels = filt.shape
    width = channels // parts
    return pl.pallas_call(
        product_kernel,
        in_specs=[VMEM] * 4,
        out_specs=VMEM,
        out_shape=jax.ShapeDtypeStruct((parts, 2 * rows, width), BF16),
        scratch_shapes=[pltpu.VMEM((2, 2, rows + 8, width), F32)],
        name="product",
    )(branches, edges, taps, filt)


def weight_copies(weight, held, sems, block):
    columns = held.shape[1]
    result = []
    for index, start in enumerate(range(0, columns, TILE)):
        span = pl.ds(pl.multiple_of(block * columns + start, TILE), TILE)
        target = held.at[:, start : start + TILE]
        result.append(pltpu.make_async_copy(weight.at[:, span], target, sems.at[index]))
    return result


def project_into(out, gated, held, copies):
    for copy, start in zip(copies, range(0, out.shape[1], TILE)):
        span = slice(start, start + TILE)
        copy.wait()
        value = jnp.dot(gated[...], held[:, span], preferred_element_type=F32)
        out[:, span] = value.astype(out.dtype)


def gate_kernel(place, mixed, branch, edges, taps, weight, gated, part, padded, held, sems):
    copies = weight_copies(weight, held, sems, place[0] ^ 3)
    for copy in copies:
        copy.start()
    parts, width = mixed.shape[0], mixed.shape[2]
    for j in range(parts):
        lanes = slice(j * width, (j + 1) * width)
        for span, second in smoothed(branch, edges.at[1], taps.at[1], lanes, padded.at[j % 2]):
            gated[span, lanes] = (second * mixed[j, span, :].astype(F32)).astype(BF16)
    project_into(part, gated, held, copies)


def rest_kernel(place, gated, weight, far_own, near_part, near_own, held, sems):
    outs = (far_own, near_part, near_own)
    sets = [
        weight_copies(weight, held.at[i], sems.at[i], place[0] ^ flip)
        for i, flip in enumerate((2, 1, 0))
    ]
    for copies in sets:
        for copy in copies:
            copy.start()
    for i, out in enumerate(outs):
        project_into(out, gated, held.at[i], sets[i])


def shards(branches, short_filter, long_filter, skip_gain, out_weight):
    seq_count, mp_count = lax.axis_size("seq"), lax.axis_size("mp")
    tokens, channels = long_filter.shape
    width = channels // seq_count
    features = out_weight.shape[1] // mp_count
    tap_count = short_filter.shape[2]
    me, place = lax.axis_index("mp"), lax.axis_index("seq")

    def exchanged(value, bit):
        return lax.ppermute(value, "mp", [(m, m ^ bit) for m in range(mp_count)])

    taps = jnp.transpose(short_filter, (0, 2, 1))
    edges = lax.ppermute(
        branches[:, tokens - (tap_count - 1) :, :],
        "seq",
        [(s, s + 1) for s in range(seq_count - 1)],
    )
    signals = product_and_filter(branches, edges, taps, long_filter, seq_count)
    signals = lax.all_to_all(signals, "seq", 0, 0, tiled=True)
    gain = lax.dynamic_slice(skip_gain, (place * width,), (width,)).reshape(1, width)
    mixed = convolve(signals, gain)
    mixed = lax.all_to_all(mixed, "seq", 0, 0, tiled=True)

    def result(dtype):
        return jax.ShapeDtypeStruct((tokens, features), dtype)

    params = pltpu.CompilerParams(vmem_limit_bytes=50 << 20)
    me = me.reshape(1)
    gated, part = pl.pallas_call(
        gate_kernel,
        in_specs=[SMEM] + [VMEM] * 4 + [HBM],
        out_specs=[VMEM] * 2,
        out_shape=[jax.ShapeDtypeStruct((tokens, channels), BF16), result(BF16)],
        scratch_shapes=[
            pltpu.VMEM((2, tokens + 8, width), F32),
            pltpu.VMEM((channels, features), BF16),
            pltpu.SemaphoreType.DMA((features // TILE,)),
        ],
        compiler_params=params,
        name="gate",
    )(me, mixed, branches[1], edges, taps, out_weight)
    other = exchanged(part, 1)
    far_own, near_part, near_own = pl.pallas_call(
        rest_kernel,
        in_specs=[SMEM, VMEM, HBM],
        out_specs=[VMEM] * 3,
        out_shape=[result(F32), result(BF16), result(F32)],
        scratch_shapes=[
            pltpu.VMEM((3, channels, features), BF16),
            pltpu.SemaphoreType.DMA((3, features // TILE)),
        ],
        compiler_params=params,
        name="rest",
    )(me, gated, out_weight)
    sent = (far_own + other.astype(F32)).astype(BF16)
    far = exchanged(sent, 2)
    near = near_own + exchanged(near_part, 1).astype(F32)
    return (near + far.astype(F32)).astype(BF16)


def solution(mesh):
    return jax.shard_map(
        shards,
        mesh=mesh,
        in_specs=(
            P(None, "seq", "mp"),
            P(None, "mp", None),
            P("seq", "mp"),
            P("mp"),
            P("mp", None),
        ),
        out_specs=P("seq", "mp"),
        check_vma=False,
    )
```

```python
import functools
import math

import jax
import jax.numpy as jnp
import numpy as np
from jax import lax
from jax.experimental import pallas as pl
from jax.experimental.pallas import tpu as pltpu
from jax.sharding import PartitionSpec as P

ROWS = 16
F32 = jnp.float32
BF16 = jnp.bfloat16


def transform_tables(length, radix):
    ids = np.arange(length)
    angle = 2.0 * math.pi * np.mod(np.outer(ids, ids), length) / length
    cosine, sine = np.cos(angle), np.sin(angle)
    matrix = np.block([[cosine, sine], [-sine, cosine]]).astype(jnp.bfloat16)
    full = length * radix
    turn = 2.0 * math.pi * np.outer(ids, np.arange(1, radix // 2 + 1)) / full
    scale = np.where(np.arange(1, radix // 2 + 1) == radix // 2, 1.0, 2.0) / full
    columns = [np.cos(turn), np.sin(turn), np.cos(turn) * scale, np.sin(turn) * scale]
    return matrix, np.concatenate(columns, axis=1).astype(np.float32)


def axpy(total, factor, value):
    if abs(factor) < 1e-9:
        return total
    if abs(factor - 1.0) < 1e-9:
        return value if total is None else total + value
    if abs(factor + 1.0) < 1e-9:
        return -value if total is None else total - value
    term = value * np.float32(factor)
    return term if total is None else total + term


def wave(step, radix):
    angle = 2.0 * math.pi * (step % radix) / radix
    return math.cos(angle), math.sin(angle)


def across_blocks(values):
    count = len(values)
    radix, half = 2 * count, count // 2
    sums = {n: values[n] + values[count - n] for n in range(1, half)}
    diffs = {n: values[n] - values[count - n] for n in range(1, half)}
    result = []
    for k in range(count + 1):
        in_cos, in_sin = (sums, diffs) if k % 2 == 0 else (diffs, sums)
        real = axpy(values[0], wave(half * k, radix)[0], values[half])
        imag = axpy(None, -wave(half * k, radix)[1], values[half])
        for n in range(1, half):
            cosine, sine = wave(n * k, radix)
            real = axpy(real, cosine, in_cos[n])
            imag = axpy(imag, -sine, in_sin[n])
        result.append((real, imag))
    return result


def back_to_blocks(first, parts):
    count = len(parts)
    radix, half = 2 * count, count // 2
    result = [None] * count
    for n in range(half + 1):
        even_cos, even_sin, odd_cos, odd_sin = first, None, None, None
        for k in range(1, count + 1):
            real, imag = parts[k - 1]
            cosine, sine = wave(n * k, radix)
            if k % 2 == 0:
                even_cos = axpy(even_cos, cosine, real)
                if imag is not None:
                    even_sin = axpy(even_sin, -sine, imag)
            else:
                odd_cos = axpy(odd_cos, cosine, real)
                odd_sin = axpy(odd_sin, -sine, imag)

        def combined(terms):
            total = None
            for sign, term in terms:
                if term is not None:
                    total = axpy(total, sign, term)
            return total

        result[n] = combined([(1, even_cos), (1, even_sin), (1, odd_cos), (1, odd_sin)])
        if 0 < n < half:
            result[count - n] = combined(
                [(1, even_cos), (-1, even_sin), (-1, odd_cos), (1, odd_sin)]
            )
    return result


VMEM = pl.BlockSpec(memory_space=pltpu.VMEM)
SMEM = pl.BlockSpec(memory_space=pltpu.SMEM)
HBM = pl.BlockSpec(memory_space=pltpu.HBM)
STRIP = 64
TILE = 512
BRANCHES = 3


def cost(flops, moved):
    return pl.CostEstimate(flops=int(flops), bytes_accessed=int(moved), transcendentals=0)


def smoothed(block, taps, lanes, padded, start, rows):
    if start == 0:
        padded[:ROWS, :] = jnp.zeros((ROWS, padded.shape[1]), F32)
    else:
        padded[:ROWS, :] = block[start - ROWS : start, lanes].astype(F32)
    strip = min(STRIP, rows)
    for begin in range(0, rows, strip):
        value = block[start + begin : start + begin + strip, lanes].astype(F32)
        padded[ROWS + begin : ROWS + begin + strip, :] = value
    for begin in range(0, rows, strip):
        total = None
        for tap in range(taps.shape[0]):
            first = ROWS - tap + begin
            term = padded[first : first + strip, :] * taps[tap : tap + 1, lanes]
            total = term if total is None else total + term
        yield slice(begin, begin + strip), total


def product_kernel(branches, taps, filt, out, padded):
    parts, width = out.shape[0], out.shape[2]
    rows, edge = filt.shape[0], taps.shape[1] - 1
    for j in range(parts):
        lanes = slice(j * width, (j + 1) * width)
        first, third = (
            smoothed(branches.at[b], taps.at[b], lanes, padded.at[j % 2, b // 2], 0, rows)
            for b in (0, 2)
        )
        for (span, left), (span, right) in zip(first, third):
            out[j, span, :] = (left * right).astype(BF16)
        out[j, rows : 2 * rows, :] = filt[:, lanes]
        rims = [branches[b, rows - ROWS :, lanes].astype(F32)[-edge:] for b in range(BRANCHES)]
        rims += [branches[b, :ROWS, lanes].astype(F32)[:edge] for b in range(BRANCHES)]
        unused = out.shape[1] - 2 * rows - 2 * BRANCHES * edge
        if unused:
            rims.append(jnp.zeros((unused, width), F32))
        out[j, 2 * rows :, :] = jnp.concatenate(rims, axis=0).astype(BF16)


def signals_of(branches, taps, filt, parts):
    rows, channels = filt.shape
    width = channels // parts
    rims = -(-2 * BRANCHES * (taps.shape[1] - 1) // ROWS) * ROWS
    return pl.pallas_call(
        product_kernel,
        in_specs=[VMEM] * 3,
        out_specs=VMEM,
        out_shape=jax.ShapeDtypeStruct((parts, 2 * rows + rims, width), BF16),
        scratch_shapes=[pltpu.VMEM((2, 2, rows + ROWS, width), F32)],
        cost_estimate=cost(40 * rows * channels, 10 * rows * channels),
        name="product",
    )(branches, taps, filt)


def chunk_of(index, offset=0):
    return pl.ds(pl.multiple_of(offset + index * ROWS, ROWS), ROWS)


def column(twist, rows, index, width):
    return jnp.broadcast_to(twist[rows, index : index + 1], (ROWS, width))


def first_rows(signals, taps, length):
    edge = taps.shape[1] - 1
    rims = signals[:, 2 * length :, :].astype(F32)
    result = []
    for branch in range(BRANCHES):
        before, after = (
            [rims[:, (side * BRANCHES + branch) * edge + i, :] for i in range(edge)]
            for side in (0, 1)
        )
        zero = jnp.zeros_like(before[0][:1])
        rows = [jnp.concatenate([zero, row[:-1]], axis=0) for row in before] + after
        smooth = []
        for i in range(edge):
            total = None
            for tap in range(edge + 1):
                term = rows[edge + i - tap] * taps[branch, tap : tap + 1, :]
                total = term if total is None else total + term
            smooth.append(total)
        result.append(smooth)
    return result


def replaced(tile, rows):
    ids = lax.broadcasted_iota(jnp.int32, tile.shape, 0)
    for i, row in enumerate(rows):
        tile = jnp.where(ids == i, jnp.broadcast_to(row, tile.shape), tile)
    return tile


def transform_kernel(matrix, twist, taps, signals, turned, product, gates, waves):
    blocks, length, width = product.shape
    pairs = blocks // 2

    smooth = first_rows(signals, taps, length)
    for b in range(blocks):
        product[b, ROWS:, :] = signals[b, ROWS:length, :]
        heads = [smooth[0][i][b : b + 1] * smooth[2][i][b : b + 1] for i in range(len(smooth[0]))]
        product[b, :ROWS, :] = replaced(signals[b, :ROWS, :].astype(F32), heads).astype(BF16)
        gains = [smooth[1][i][b : b + 1] for i in range(len(smooth[1]))]
        gates[b] = replaced(jnp.ones((ROWS, width), F32), gains)

    def forward(index, carry):
        rows, low = chunk_of(index), chunk_of(index, length)
        for side in (0, 1):
            lanes = slice(side * width, (side + 1) * width)
            if side == 0:
                values = [product[b, rows, :].astype(F32) for b in range(blocks)]
            else:
                values = [signals[b, low, :].astype(F32) for b in range(blocks)]
            spectra = across_blocks(values)
            waves[0, rows, lanes] = spectra[0][0].astype(BF16)
            for k in range(1, blocks + 1):
                real, imag = spectra[k]
                cosine = column(twist, rows, k - 1, width)
                sine = column(twist, rows, blocks + k - 1, width)
                if imag is None:
                    waves[k, rows, lanes] = (real * cosine).astype(BF16)
                    waves[k, low, lanes] = (-real * sine).astype(BF16)
                else:
                    waves[k, rows, lanes] = (real * cosine + imag * sine).astype(BF16)
                    waves[k, low, lanes] = (imag * cosine - real * sine).astype(BF16)
        return carry

    lax.fori_loop(0, length // ROWS, forward, 0)

    def multiplied(spectrum):
        real, imag = spectrum[:length], spectrum[length:]
        a_real, a_imag = real[:, :width], imag[:, :width]
        b_real, b_imag = real[:, width:], imag[:, width:]
        return jnp.concatenate(
            [
                (a_real * b_real - a_imag * b_imag).astype(BF16),
                (-(a_real * b_imag + a_imag * b_real)).astype(BF16),
            ],
            axis=0,
        )

    def dot(left, right):
        return jnp.dot(left, right, preferred_element_type=F32)

    base = multiplied(dot(matrix[:, :length], waves[0, :length, :]))
    turned[pairs, :length, :width] = dot(matrix[:length, :], base)

    def one_pair(pair):
        left = multiplied(dot(matrix[...], waves[2 * pair + 1]))
        right = multiplied(dot(matrix[...], waves[2 * pair + 2]))
        turned[pair] = dot(matrix[...], jnp.concatenate([left, right], axis=1))

    if pairs <= 4:
        for pair in range(pairs):
            one_pair(pair)
    else:
        lax.fori_loop(0, pairs, lambda pair, carry: (one_pair(pair), carry)[1], 0)


def back_kernel(start, twist, gain, gates, turned, product, out):
    blocks, count, width = out.shape
    length = product.shape[1]
    full, pairs = 2 * blocks * length, blocks // 2
    skip = jnp.broadcast_to(gain[...], (ROWS, width))

    def backward(index, carry):
        rows, low = chunk_of(index, start), chunk_of(index, length + start)
        parts = []
        for k in range(1, blocks + 1):
            pair, side = (k - 1) // 2, (k - 1) % 2
            lanes = slice(side * width, (side + 1) * width)
            real, minus = turned[pair, rows, lanes], turned[pair, low, lanes]
            cosine = column(twist, rows, 2 * blocks + k - 1, width)
            sine = column(twist, rows, 3 * blocks + k - 1, width)
            turned_real = real * cosine + minus * sine
            parts.append((turned_real, None if k == blocks else real * sine - minus * cosine))
        first = turned[pairs, rows, :width] * np.float32(1.0 / full)
        for b, value in enumerate(back_to_blocks(first, parts)):
            direct = skip * product[b, rows, :].astype(F32)
            out[b, chunk_of(index), :] = (value + direct).astype(BF16)
        return carry

    lax.fori_loop(0, count // ROWS, backward, 0)
    if start == 0:
        for b in range(blocks):
            out[b, :ROWS, :] = (out[b, :ROWS, :].astype(F32) * gates[b]).astype(BF16)


def weight_copies(weight, held, sems, block):
    columns = held.shape[1]
    result = []
    for index, start in enumerate(range(0, columns, TILE)):
        span = pl.ds(pl.multiple_of(block * columns + start, TILE), TILE)
        target = held.at[:, start : start + TILE]
        result.append(pltpu.make_async_copy(weight.at[:, span], target, sems.at[index]))
    return result


def project_into(out, gated, held, copies):
    for copy, start in zip(copies, range(0, out.shape[1], TILE)):
        span = slice(start, start + TILE)
        copy.wait()
        value = jnp.dot(gated, held[:, span], preferred_element_type=F32)
        out[:, span] = value.astype(out.dtype)


def gate_kernel(start, place, mixed, branch, taps, weight, gated, part, padded, held, sems):
    copies = weight_copies(weight, held, sems, place[0] ^ 3)
    for copy in copies:
        copy.start()
    parts, rows, width = mixed.shape
    for j in range(parts):
        lanes = slice(j * width, (j + 1) * width)
        strips = smoothed(branch, taps.at[1], lanes, padded.at[j % 2], start, rows)
        for span, second in strips:
            value = mixed[j, span, :].astype(F32)
            done = second * value
            if start == 0 and span.start == 0:
                ids = lax.broadcasted_iota(jnp.int32, done.shape, 0)
                done = jnp.where(ids < taps.shape[1] - 1, value, done)
            gated[span, lanes] = done.astype(BF16)
    project_into(part, gated[...], held, copies)


def own_kernel(place, gated, weight, own, held, sems):
    copies = weight_copies(weight, held, sems, place[0] ^ 2)
    for copy in copies:
        copy.start()
    project_into(own, gated[...], held, copies)


def near_kernel(place, gated, weight, part, own, held, sems):
    sets = [weight_copies(weight, held.at[i], sems.at[i], place[0] ^ (1 - i)) for i in (0, 1)]
    for copies in sets:
        for copy in copies:
            copy.start()
    for i, out in enumerate((part, own)):
        project_into(out, gated[...], held.at[i], sets[i])


def shards(branches, short_filter, long_filter, skip_gain, out_weight):
    seq_count, mp_count = lax.axis_size("seq"), lax.axis_size("mp")
    tokens, channels = long_filter.shape
    width = channels // seq_count
    features = out_weight.shape[1] // mp_count
    me, place = lax.axis_index("mp").reshape(1), lax.axis_index("seq")
    params = pltpu.CompilerParams(vmem_limit_bytes=50 << 20)
    small = pltpu.CompilerParams(vmem_limit_bytes=24 << 20)
    half = tokens
    starts = (0,)

    def exchanged(value, bit):
        return lax.ppermute(value, "mp", [(m, m ^ bit) for m in range(mp_count)])

    def across(value):
        return lax.all_to_all(value, "seq", 0, 0, tiled=True)

    def shape(rows, dtype):
        return jax.ShapeDtypeStruct((rows, features), dtype)

    taps = jnp.transpose(short_filter, (0, 2, 1))
    signals = across(signals_of(branches, taps, long_filter, seq_count))

    mine = place * width
    gain = lax.dynamic_slice(skip_gain, (mine,), (width,)).reshape(1, width)
    my_taps = lax.dynamic_slice_in_dim(taps, mine, width, 2)
    matrix, twist = (jnp.asarray(t) for t in transform_tables(tokens, 2 * seq_count))
    turned, product, gates = pl.pallas_call(
        transform_kernel,
        in_specs=[VMEM] * 4,
        out_specs=[VMEM] * 3,
        out_shape=[
            jax.ShapeDtypeStruct((seq_count // 2 + 1, 2 * tokens, 2 * width), F32),
            jax.ShapeDtypeStruct((seq_count, tokens, width), BF16),
            jax.ShapeDtypeStruct((seq_count, ROWS, width), F32),
        ],
        scratch_shapes=[pltpu.VMEM((seq_count + 1, 2 * tokens, 2 * width), BF16)],
        compiler_params=small,
        cost_estimate=cost(seq_count * 12 * (2 * tokens) ** 2 * width, 6 << 20),
        name="transform",
    )(matrix, twist, my_taps, signals)
    mixed = []
    for start in starts:
        part = pl.pallas_call(
            functools.partial(back_kernel, start),
            in_specs=[VMEM] * 5,
            out_specs=VMEM,
            out_shape=jax.ShapeDtypeStruct((seq_count, half, width), BF16),
            compiler_params=small,
            cost_estimate=cost(200 * tokens * channels, 5 << 20),
            name="back",
        )(twist, gain, gates, turned, product)
        mixed.append(across(part))

    held = [
        pltpu.VMEM((channels, features), BF16),
        pltpu.SemaphoreType.DMA((features // TILE,)),
    ]
    gated, far = [], []
    for start, value in zip(starts, mixed):
        ready, part = pl.pallas_call(
            functools.partial(gate_kernel, start),
            in_specs=[SMEM] + [VMEM] * 3 + [HBM],
            out_specs=[VMEM] * 2,
            out_shape=[jax.ShapeDtypeStruct((half, channels), BF16), shape(half, BF16)],
            scratch_shapes=[pltpu.VMEM((2, half + ROWS, width), F32)] + held,
            compiler_params=params,
            cost_estimate=cost(2 * tokens * channels * features, 2 * channels * features),
            name="gate",
        )(me, value, branches[1], taps, out_weight)
        other = exchanged(part, 1)
        own = pl.pallas_call(
            own_kernel,
            in_specs=[SMEM, VMEM, HBM],
            out_specs=VMEM,
            out_shape=shape(half, F32),
            scratch_shapes=held,
            compiler_params=params,
            cost_estimate=cost(2 * tokens * channels * features, 2 * channels * features),
            name="own",
        )(me, ready, out_weight)
        sent = (own + other.astype(F32)).astype(BF16)
        gated.append(ready)
        far.append(exchanged(sent, 2))
    gated[0], sent = lax.optimization_barrier((gated[0], sent))
    near_part, near_own = pl.pallas_call(
        near_kernel,
        in_specs=[SMEM, VMEM, HBM],
        out_specs=[VMEM] * 2,
        out_shape=[shape(tokens, BF16), shape(tokens, F32)],
        scratch_shapes=[
            pltpu.VMEM((2, channels, features), BF16),
            pltpu.SemaphoreType.DMA((2, features // TILE)),
        ],
        compiler_params=params,
        cost_estimate=cost(4 * tokens * channels * features, 4 * channels * features),
        name="near",
    )(me, *gated, out_weight)
    near = near_own + exchanged(near_part, 1).astype(F32)
    return (near + far[0].astype(F32)).astype(BF16)


def solution(mesh):
    return jax.shard_map(
        shards,
        mesh=mesh,
        in_specs=(
            P(None, "seq", "mp"),
            P(None, "mp", None),
            P("seq", "mp"),
            P("mp"),
            P("mp", None),
        ),
        out_specs=P("seq", "mp"),
        check_vma=False,
    )
```

```python
import functools
import math

import jax
import jax.numpy as jnp
import numpy as np
from jax import lax
from jax.experimental import pallas as pl
from jax.experimental.pallas import tpu as pltpu
from jax.sharding import PartitionSpec as P

ROWS = 16
F32 = jnp.float32
BF16 = jnp.bfloat16


def transform_tables(length, radix):
    ids = np.arange(length)
    angle = 2.0 * math.pi * np.mod(np.outer(ids, ids), length) / length
    cosine, sine = np.cos(angle), np.sin(angle)
    matrix = np.block([[cosine, sine], [-sine, cosine]]).astype(jnp.bfloat16)
    full = length * radix
    turn = 2.0 * math.pi * np.outer(ids, np.arange(1, radix // 2 + 1)) / full
    scale = np.where(np.arange(1, radix // 2 + 1) == radix // 2, 1.0, 2.0) / full
    columns = [np.cos(turn), np.sin(turn), np.cos(turn) * scale, np.sin(turn) * scale]
    return matrix, np.concatenate(columns, axis=1).astype(np.float32)


def axpy(total, factor, value):
    if abs(factor) < 1e-9:
        return total
    if abs(factor - 1.0) < 1e-9:
        return value if total is None else total + value
    if abs(factor + 1.0) < 1e-9:
        return -value if total is None else total - value
    term = value * np.float32(factor)
    return term if total is None else total + term


def wave(step, radix):
    angle = 2.0 * math.pi * (step % radix) / radix
    return math.cos(angle), math.sin(angle)


def combined(signs, terms):
    total = None
    for sign, term in zip(signs, terms):
        if term is not None:
            total = axpy(total, sign, term)
    return total


def across_blocks(values):
    count = len(values)
    radix, half = 2 * count, count // 2
    sums = {n: values[n] + values[count - n] for n in range(1, half)}
    diffs = {n: values[n] - values[count - n] for n in range(1, half)}
    result = [None] * (count + 1)
    for k in range(half + 1):
        in_cos, in_sin = (sums, diffs) if k % 2 == 0 else (diffs, sums)
        real = [axpy(values[0], wave(half * k, radix)[0], values[half]), None]
        imag = [axpy(None, -wave(half * k, radix)[1], values[half]), None]
        for n in range(1, half):
            cosine, sine = wave(n * k, radix)
            real[n % 2] = axpy(real[n % 2], cosine, in_cos[n])
            imag[n % 2] = axpy(imag[n % 2], -sine, in_sin[n])
        result[k] = (combined([1, 1], real), combined([1, 1], imag))
        if k < half:
            result[count - k] = (combined([1, -1], real), combined([-1, 1], imag))
    return result


def back_to_blocks(first, parts):
    count = len(parts)
    radix, half = 2 * count, count // 2
    result = [None] * count
    for n in range(half + 1):
        even_cos, even_sin, odd_cos, odd_sin = first, None, None, None
        for k in range(1, count + 1):
            real, imag = parts[k - 1]
            cosine, sine = wave(n * k, radix)
            if k % 2 == 0:
                even_cos = axpy(even_cos, cosine, real)
                if imag is not None:
                    even_sin = axpy(even_sin, -sine, imag)
            else:
                odd_cos = axpy(odd_cos, cosine, real)
                odd_sin = axpy(odd_sin, -sine, imag)

        terms = (even_cos, even_sin, odd_cos, odd_sin)
        result[n] = combined((1, 1, 1, 1), terms)
        if 0 < n < half:
            result[count - n] = combined((1, -1, -1, 1), terms)
    return result


VMEM = pl.BlockSpec(memory_space=pltpu.VMEM)
SMEM = pl.BlockSpec(memory_space=pltpu.SMEM)
HBM = pl.BlockSpec(memory_space=pltpu.HBM)
TILE = 512
PIECES = 8
STEPS = 4
BRANCHES = 3


def cost(flops, moved):
    return pl.CostEstimate(flops=int(flops), bytes_accessed=int(moved), transcendentals=0)


def smoothed(block, lanes, taps, padded, rows, start=0):
    if start == 0:
        padded[:ROWS, :] = jnp.zeros((ROWS, padded.shape[1]), F32)
    else:
        padded[:ROWS, :] = block[start - ROWS : start, lanes].astype(F32)
    strip = next(n for n in (64, 32, 16) if rows % n == 0)
    for begin in range(0, rows, strip):
        value = block[start + begin : start + begin + strip, lanes].astype(F32)
        padded[ROWS + begin : ROWS + begin + strip, :] = value
    for begin in range(0, rows, strip):
        total = None
        for tap in range(len(taps)):
            first = ROWS - tap + begin
            term = padded[first : first + strip, :] * taps[tap]
            total = term if total is None else total + term
        yield slice(begin, begin + strip), total


def tap_rows(taps, branch, lanes):
    return [taps[branch, tap : tap + 1, lanes] for tap in range(taps.shape[1])]


def product_kernel(all_taps, branches, filt, out, taps, held, rims, ready, padded, ins, ends, outs):
    parts, height, width = out.shape
    rows, edge = filt.shape[0], taps.shape[1] - 1
    copies = [pltpu.make_async_copy(all_taps, taps, ends.at[2])]
    for side in (0, 1):
        source = branches.at[1, pl.ds(side * (rows - ROWS), ROWS), :]
        copies.append(pltpu.make_async_copy(source, rims.at[side], ends.at[side]))
    for i, source in enumerate((branches.at[0], branches.at[2], filt)):
        copies.append(pltpu.make_async_copy(source, held.at[i], ins.at[i]))
    for copy in copies:
        copy.start()
    for copy in copies:
        copy.wait()
    first, third, kept = (held.at[i] for i in range(3))
    sent = []
    for j in range(parts):
        lanes = slice(j * width, (j + 1) * width)
        pair = (
            smoothed(block, lanes, tap_rows(taps, b, lanes), padded.at[j % 2, b // 2], rows)
            for block, b in ((first, 0), (third, 2))
        )
        for (span, left), (span, right) in zip(*pair):
            ready[j, span, :] = (left * right).astype(BF16)
        ready[j, rows : 2 * rows, :] = kept[:, lanes]
        tails = [
            first[rows - ROWS :, lanes].astype(F32)[-edge:],
            rims[1, :, lanes].astype(F32)[-edge:],
            third[rows - ROWS :, lanes].astype(F32)[-edge:],
            first[:ROWS, lanes].astype(F32)[:edge],
            rims[0, :, lanes].astype(F32)[:edge],
            third[:ROWS, lanes].astype(F32)[:edge],
        ]
        unused = height - 2 * rows - 2 * BRANCHES * edge
        if unused:
            tails.append(jnp.zeros((unused, width), F32))
        ready[j, 2 * rows :, :] = jnp.concatenate(tails, axis=0).astype(BF16)
        copy = pltpu.make_async_copy(ready.at[j], out.at[j], outs.at[j])
        copy.start()
        sent.append(copy)
    for copy in sent:
        copy.wait()


def signals_of(branches, taps, filt, parts):
    rows, channels = filt.shape
    width = channels // parts
    height = 2 * rows - (-2 * BRANCHES * (taps.shape[1] - 1) // ROWS) * ROWS
    return pl.pallas_call(
        product_kernel,
        in_specs=[HBM] * 3,
        out_specs=HBM,
        out_shape=jax.ShapeDtypeStruct((parts, height, width), BF16),
        scratch_shapes=[
            pltpu.VMEM(taps.shape, F32),
            pltpu.VMEM((3, rows, channels), BF16),
            pltpu.VMEM((2, ROWS, channels), BF16),
            pltpu.VMEM((parts, height, width), BF16),
            pltpu.VMEM((2, 2, rows + ROWS, width), F32),
            pltpu.SemaphoreType.DMA((3,)),
            pltpu.SemaphoreType.DMA((3,)),
            pltpu.SemaphoreType.DMA((parts,)),
        ],
        compiler_params=pltpu.CompilerParams(vmem_limit_bytes=62 << 20),
        cost_estimate=cost(40 * rows * channels, 10 * rows * channels),
        name="product",
    )(taps, branches, filt)


def unrolled(blocks):
    return 4 if blocks <= 8 else 1


def chunk_of(index, offset=0):
    return pl.ds(pl.multiple_of(offset + index * ROWS, ROWS), ROWS)


def column(twist, rows, index, width):
    return jnp.broadcast_to(twist[rows, index : index + 1], (ROWS, width))


def first_rows(signals, taps, length):
    edge = taps.shape[1] - 1
    rims = signals[:, 2 * length :, :].astype(F32)
    result = []
    for branch in range(BRANCHES):
        before, after = (
            [rims[:, (side * BRANCHES + branch) * edge + i, :] for i in range(edge)]
            for side in (0, 1)
        )
        zero = jnp.zeros_like(before[0][:1])
        rows = [jnp.concatenate([zero, row[:-1]], axis=0) for row in before] + after
        smooth = []
        for i in range(edge):
            total = None
            for tap in range(edge + 1):
                term = rows[edge + i - tap] * taps[branch, tap : tap + 1, :]
                total = term if total is None else total + term
            smooth.append(total)
        result.append(smooth)
    return result


def replaced(tile, rows):
    ids = lax.broadcasted_iota(jnp.int32, tile.shape, 0)
    for i, row in enumerate(rows):
        tile = jnp.where(ids == i, jnp.broadcast_to(row, tile.shape), tile)
    return tile


def transform_kernel(matrix, twist, taps, signals, turned, product, gates, waves):
    blocks, length, width = product.shape
    pairs = blocks // 2

    smooth = first_rows(signals, taps, length)
    for b in range(blocks):
        product[b, ROWS:, :] = signals[b, ROWS:length, :]
        heads = [smooth[0][i][b : b + 1] * smooth[2][i][b : b + 1] for i in range(len(smooth[0]))]
        product[b, :ROWS, :] = replaced(signals[b, :ROWS, :].astype(F32), heads).astype(BF16)
        gains = [smooth[1][i][b : b + 1] for i in range(len(smooth[1]))]
        gates[b] = replaced(jnp.ones((ROWS, width), F32), gains)

    def forward(index, carry):
        rows, low = chunk_of(index), chunk_of(index, length)
        turns = [
            (column(twist, rows, k, width), column(twist, rows, blocks + k, width))
            for k in range(blocks)
        ]
        for side in (0, 1):
            lanes = slice(side * width, (side + 1) * width)
            if side == 0:
                values = [product[b, rows, :].astype(F32) for b in range(blocks)]
            else:
                values = [signals[b, low, :].astype(F32) for b in range(blocks)]
            spectra = across_blocks(values)
            waves[0, rows, lanes] = spectra[0][0].astype(BF16)
            for k in range(1, blocks + 1):
                real, imag = spectra[k]
                cosine, sine = turns[k - 1]
                if imag is None:
                    waves[k, rows, lanes] = (real * cosine).astype(BF16)
                    waves[k, low, lanes] = (-real * sine).astype(BF16)
                else:
                    waves[k, rows, lanes] = (real * cosine + imag * sine).astype(BF16)
                    waves[k, low, lanes] = (imag * cosine - real * sine).astype(BF16)
        return carry

    lax.fori_loop(0, length // ROWS, forward, 0, unroll=unrolled(blocks))

    def multiplied(spectrum):
        real, imag = spectrum[:length], spectrum[length:]
        a_real, a_imag = real[:, :width], imag[:, :width]
        b_real, b_imag = real[:, width:], imag[:, width:]
        return jnp.concatenate(
            [
                (a_real * b_real - a_imag * b_imag).astype(BF16),
                (-(a_real * b_imag + a_imag * b_real)).astype(BF16),
            ],
            axis=0,
        )

    def dot(left, right):
        return jnp.dot(left, right, preferred_element_type=F32)

    base = multiplied(dot(matrix[:, :length], waves[0, :length, :]))
    turned[pairs, :length, :width] = dot(matrix[:length, :], base)

    def one_pair(pair):
        left = multiplied(dot(matrix[...], waves[2 * pair + 1]))
        right = multiplied(dot(matrix[...], waves[2 * pair + 2]))
        turned[pair] = dot(matrix[...], jnp.concatenate([left, right], axis=1))

    if pairs <= 4:
        for pair in range(pairs):
            one_pair(pair)
    else:
        lax.fori_loop(0, pairs, lambda pair, carry: (one_pair(pair), carry)[1], 0)


def back_kernel(twist, gain, gates, turned, product, *outs):
    blocks, length, width = product.shape
    full, pairs = 2 * blocks * length, blocks // 2
    skip = jnp.broadcast_to(gain[...], (ROWS, width))

    def backward(out, start, index, carry):
        rows, low = chunk_of(index, start), chunk_of(index, length + start)
        parts = []
        for k in range(1, blocks + 1):
            pair, side = (k - 1) // 2, (k - 1) % 2
            lanes = slice(side * width, (side + 1) * width)
            real, minus = turned[pair, rows, lanes], turned[pair, low, lanes]
            cosine = column(twist, rows, 2 * blocks + k - 1, width)
            sine = column(twist, rows, 3 * blocks + k - 1, width)
            turned_real = real * cosine + minus * sine
            parts.append((turned_real, None if k == blocks else real * sine - minus * cosine))
        first = turned[pairs, rows, :width] * np.float32(1.0 / full)
        for b, value in enumerate(back_to_blocks(first, parts)):
            direct = skip * product[b, rows, :].astype(F32)
            out[b, chunk_of(index), :] = (value + direct).astype(BF16)
        return carry

    start = 0
    for out in outs:
        body = functools.partial(backward, out, start)
        lax.fori_loop(0, out.shape[1] // ROWS, body, 0, unroll=unrolled(blocks))
        start += out.shape[1]
    for b in range(blocks):
        outs[0][b, :ROWS, :] = (outs[0][b, :ROWS, :].astype(F32) * gates[b]).astype(BF16)


def weight_copies(weight, held, sems, block):
    depth, columns = held.shape
    span = pl.ds(pl.multiple_of(block * columns, columns), columns)
    step = depth // PIECES
    pieces = [pl.ds(i * step, step) for i in range(PIECES)]
    return [
        pltpu.make_async_copy(weight.at[rows, span], held.at[rows, :], sems.at[i])
        for i, rows in enumerate(pieces)
    ]


def start_all(copies):
    for copy in copies:
        copy.start()


def project_into(outs, gated, weight, copies, total):
    depth, columns = weight.shape
    group = PIECES // STEPS
    for step in range(STEPS):
        for copy in copies[step * group : (step + 1) * group]:
            copy.wait()
        rows = slice(step * depth // STEPS, (step + 1) * depth // STEPS)
        for start in range(0, columns, TILE):
            span = slice(start, start + TILE)
            value = jnp.dot(gated[:, rows], weight[rows, span], preferred_element_type=F32)
            if step:
                value = total[:, span] + value
            if step < STEPS - 1:
                total[:, span] = value
            else:
                index, offset = divmod(start, columns // len(outs))
                out = outs[index]
                out[:, offset : offset + TILE] = value.astype(out.dtype)


def gated_rows(start, mixed, branch, taps, gated, padded):
    parts, rows, width = mixed.shape
    for j in range(parts):
        lanes = slice(j * width, (j + 1) * width)
        strips = smoothed(branch, lanes, tap_rows(taps, 1, lanes), padded.at[j % 2], rows, start)
        for span, second in strips:
            value = mixed[j, span, :].astype(F32)
            done = second * value
            if start == 0 and span.start == 0:
                ids = lax.broadcasted_iota(jnp.int32, done.shape, 0)
                done = jnp.where(ids < taps.shape[1] - 1, value, done)
            gated[span, lanes] = done.astype(BF16)


def gate_kernel(start, place, mixed, branch, taps, weight, gated, part, padded, held, sems, total):
    copies = weight_copies(weight, held.at[0], sems.at[0], place[0] ^ 3)
    start_all(copies)
    gated_rows(start, mixed, branch, taps, gated, padded)
    project_into([part], gated, held.at[0], copies, total)


def own_kernel(place, gated, weight, own, held, sems, total):
    copies = weight_copies(weight, held.at[0], sems.at[0], place[0] ^ 2)
    start_all(copies)
    project_into([own], gated, held.at[0], copies, total)


def near_kernel(place, first, second, weight, *rest):
    *parts, own, held, sems, total, gated = rest
    sets = [weight_copies(weight, held.at[i], sems.at[i], place[0] ^ (1 - i)) for i in (0, 1)]
    start_all(sets[0])
    start_all(sets[1])
    rows = first.shape[0]
    gated[:rows, :] = first[...]
    gated[rows:, :] = second[...]
    project_into(parts, gated, held.at[0], sets[0], total)
    project_into([own], gated, held.at[1], sets[1], total)


def shards(branches, short_filter, long_filter, skip_gain, out_weight):
    seq_count, mp_count = lax.axis_size("seq"), lax.axis_size("mp")
    tokens, channels = long_filter.shape
    width = channels // seq_count
    features = out_weight.shape[1] // mp_count
    me, place = lax.axis_index("mp").reshape(1), lax.axis_index("seq")
    params = pltpu.CompilerParams(vmem_limit_bytes=50 << 20)
    small = pltpu.CompilerParams(vmem_limit_bytes=24 << 20)

    def exchanged(value, bit):
        return lax.ppermute(value, "mp", [(m, m ^ bit) for m in range(mp_count)])

    def across(value):
        return lax.all_to_all(value, "seq", 0, 0, tiled=True)

    def shape(dtype, rows):
        return jax.ShapeDtypeStruct((rows, features), dtype)

    taps = jnp.transpose(short_filter, (0, 2, 1))
    signals = across(signals_of(branches, taps, long_filter, seq_count))

    mine = place * width
    gain = lax.dynamic_slice(skip_gain, (mine,), (width,)).reshape(1, width)
    my_taps = lax.dynamic_slice_in_dim(taps, mine, width, 2)
    matrix, twist = (jnp.asarray(t) for t in transform_tables(tokens, 2 * seq_count))
    turned, product, gates = pl.pallas_call(
        transform_kernel,
        in_specs=[VMEM] * 4,
        out_specs=[VMEM] * 3,
        out_shape=[
            jax.ShapeDtypeStruct((seq_count // 2 + 1, 2 * tokens, 2 * width), F32),
            jax.ShapeDtypeStruct((seq_count, tokens, width), BF16),
            jax.ShapeDtypeStruct((seq_count, ROWS, width), F32),
        ],
        scratch_shapes=[pltpu.VMEM((seq_count + 1, 2 * tokens, 2 * width), BF16)],
        compiler_params=small,
        cost_estimate=cost(seq_count * 12 * (2 * tokens) ** 2 * width, 6 << 20),
        name="transform",
    )(matrix, twist, my_taps, signals)
    counts = (tokens * 128 // 256, tokens * 128 // 256)
    mixed = pl.pallas_call(
        back_kernel,
        in_specs=[VMEM] * 5,
        out_specs=[VMEM] * len(counts),
        out_shape=[jax.ShapeDtypeStruct((seq_count, count, width), BF16) for count in counts],
        compiler_params=small,
        cost_estimate=cost(200 * tokens * channels, 5 << 20),
        name="back",
    )(twist, gain, gates, turned, product)
    mixed = [across(part) for part in mixed]

    flops, moved = 2 * tokens * channels * features, 2 * channels * features
    held = pltpu.VMEM((2, channels, features), BF16)
    sems = pltpu.SemaphoreType.DMA((2, PIECES))
    gated, far = [], []
    start = 0
    for step, (value, count) in enumerate(zip(mixed, counts)):
        padded = pltpu.VMEM((2, count + ROWS, width), F32)
        total = pltpu.VMEM((count, features), F32)
        if step:
            value, sent = lax.optimization_barrier((value, sent))
        ready, part = pl.pallas_call(
            functools.partial(gate_kernel, start),
            in_specs=[SMEM] + [VMEM] * 3 + [HBM],
            out_specs=[VMEM] * 2,
            out_shape=[jax.ShapeDtypeStruct((count, channels), BF16), shape(BF16, count)],
            scratch_shapes=[padded, held, sems, total],
            compiler_params=params,
            cost_estimate=cost(1, 1),
            name="gate",
        )(me, value, branches[1], taps, out_weight)
        other = exchanged(part, 1)
        own = pl.pallas_call(
            own_kernel,
            in_specs=[SMEM, VMEM, HBM],
            out_specs=VMEM,
            out_shape=shape(F32, count),
            scratch_shapes=[held, sems, total],
            compiler_params=params,
            cost_estimate=cost(1, 1),
            name="own",
        )(me, ready, out_weight)
        if step:
            own, far[0] = lax.optimization_barrier((own, far[0]))
        sent = (own + other.astype(F32)).astype(BF16)
        gated.append(ready)
        far.append(exchanged(sent, 2))
        start += count
    gated[0], gated[1], sent = lax.optimization_barrier((gated[0], gated[1], sent))
    pieces = 4
    *near_part, near_own = pl.pallas_call(
        near_kernel,
        in_specs=[SMEM, VMEM, VMEM, HBM],
        out_specs=[VMEM] * (pieces + 1),
        out_shape=[jax.ShapeDtypeStruct((tokens, features // pieces), BF16)] * pieces
        + [shape(F32, tokens)],
        scratch_shapes=[
            held,
            sems,
            pltpu.VMEM((tokens, features), F32),
            pltpu.VMEM((tokens, channels), BF16),
        ],
        compiler_params=params,
        cost_estimate=cost(1, 1),
        name="near",
    )(me, *gated, out_weight)
    near_part = jnp.concatenate([exchanged(part, 1) for part in near_part], axis=1)
    near = near_own + near_part.astype(F32)
    return (near + jnp.concatenate(far, axis=0).astype(F32)).astype(BF16)


def solution(mesh):
    return jax.shard_map(
        shards,
        mesh=mesh,
        in_specs=(
            P(None, "seq", "mp"),
            P(None, "mp", None),
            P("seq", "mp"),
            P("mp"),
            P("mp", None),
        ),
        out_specs=P("seq", "mp"),
        check_vma=False,
    )
```

```python
import functools
import math

import jax
import jax.numpy as jnp
import numpy as np
from jax import lax
from jax.experimental import pallas as pl
from jax.experimental.pallas import tpu as pltpu
from jax.sharding import PartitionSpec as P

ROWS = 16
F32 = jnp.float32
BF16 = jnp.bfloat16


def transform_tables(length, radix):
    ids = np.arange(length)
    angle = 2.0 * math.pi * np.mod(np.outer(ids, ids), length) / length
    cosine, sine = np.cos(angle), np.sin(angle)
    matrix = np.block([[cosine, sine], [-sine, cosine]]).astype(jnp.bfloat16)
    full = length * radix
    turn = 2.0 * math.pi * np.outer(ids, np.arange(1, radix // 2 + 1)) / full
    scale = np.where(np.arange(1, radix // 2 + 1) == radix // 2, 1.0, 2.0) / full
    columns = [np.cos(turn), np.sin(turn), np.cos(turn) * scale, np.sin(turn) * scale]
    return matrix, np.concatenate(columns, axis=1).astype(np.float32)


def axpy(total, factor, value):
    if abs(factor) < 1e-9:
        return total
    if abs(factor - 1.0) < 1e-9:
        return value if total is None else total + value
    if abs(factor + 1.0) < 1e-9:
        return -value if total is None else total - value
    term = value * np.float32(factor)
    return term if total is None else total + term


def wave(step, radix):
    angle = 2.0 * math.pi * (step % radix) / radix
    return math.cos(angle), math.sin(angle)


def combined(signs, terms):
    total = None
    for sign, term in zip(signs, terms):
        if term is not None:
            total = axpy(total, sign, term)
    return total


def across_blocks(values):
    count = len(values)
    radix, half = 2 * count, count // 2
    sums = {n: values[n] + values[count - n] for n in range(1, half)}
    diffs = {n: values[n] - values[count - n] for n in range(1, half)}
    result = [None] * (count + 1)
    for k in range(half + 1):
        in_cos, in_sin = (sums, diffs) if k % 2 == 0 else (diffs, sums)
        real = [axpy(values[0], wave(half * k, radix)[0], values[half]), None]
        imag = [axpy(None, -wave(half * k, radix)[1], values[half]), None]
        for n in range(1, half):
            cosine, sine = wave(n * k, radix)
            real[n % 2] = axpy(real[n % 2], cosine, in_cos[n])
            imag[n % 2] = axpy(imag[n % 2], -sine, in_sin[n])
        result[k] = (combined([1, 1], real), combined([1, 1], imag))
        if k < half:
            result[count - k] = (combined([1, -1], real), combined([-1, 1], imag))
    return result


def back_to_blocks(first, parts):
    count = len(parts)
    radix, half = 2 * count, count // 2
    result = [None] * count
    for n in range(half + 1):
        even_cos, even_sin, odd_cos, odd_sin = first, None, None, None
        for k in range(1, count + 1):
            real, imag = parts[k - 1]
            cosine, sine = wave(n * k, radix)
            if k % 2 == 0:
                even_cos = axpy(even_cos, cosine, real)
                if imag is not None:
                    even_sin = axpy(even_sin, -sine, imag)
            else:
                odd_cos = axpy(odd_cos, cosine, real)
                odd_sin = axpy(odd_sin, -sine, imag)

        terms = (even_cos, even_sin, odd_cos, odd_sin)
        result[n] = combined((1, 1, 1, 1), terms)
        if 0 < n < half:
            result[count - n] = combined((1, -1, -1, 1), terms)
    return result


VMEM = pl.BlockSpec(memory_space=pltpu.VMEM)
SMEM = pl.BlockSpec(memory_space=pltpu.SMEM)
HBM = pl.BlockSpec(memory_space=pltpu.HBM)
TILE = 512
PIECES = 8
STEPS = 4
BRANCHES = 3


def cost(flops, moved):
    return pl.CostEstimate(flops=int(flops), bytes_accessed=int(moved), transcendentals=0)


def smoothed(block, lanes, taps, padded, rows, start=0):
    if start == 0:
        padded[:ROWS, :] = jnp.zeros((ROWS, padded.shape[1]), F32)
    else:
        padded[:ROWS, :] = block[start - ROWS : start, lanes].astype(F32)
    strip = next(n for n in (64, 32, 16) if rows % n == 0)
    for begin in range(0, rows, strip):
        value = block[start + begin : start + begin + strip, lanes].astype(F32)
        padded[ROWS + begin : ROWS + begin + strip, :] = value
    for begin in range(0, rows, strip):
        total = None
        for tap in range(len(taps)):
            first = ROWS - tap + begin
            term = padded[first : first + strip, :] * taps[tap]
            total = term if total is None else total + term
        yield slice(begin, begin + strip), total


def tap_rows(taps, branch, lanes):
    return [taps[branch, tap : tap + 1, lanes] for tap in range(taps.shape[1])]


def product_kernel(all_taps, branches, filt, out, taps, held, rims, ready, padded, ins, ends, outs):
    parts, height, width = out.shape
    rows, edge = filt.shape[0], taps.shape[1] - 1
    copies = [pltpu.make_async_copy(all_taps, taps, ends.at[2])]
    for side in (0, 1):
        source = branches.at[1, pl.ds(side * (rows - ROWS), ROWS), :]
        copies.append(pltpu.make_async_copy(source, rims.at[side], ends.at[side]))
    for i, source in enumerate((branches.at[0], branches.at[2], filt)):
        copies.append(pltpu.make_async_copy(source, held.at[i], ins.at[i]))
    for copy in copies:
        copy.start()
    for copy in copies:
        copy.wait()
    first, third, kept = (held.at[i] for i in range(3))
    sent = []
    for j in range(parts):
        lanes = slice(j * width, (j + 1) * width)
        pair = (
            smoothed(block, lanes, tap_rows(taps, b, lanes), padded.at[j % 2, b // 2], rows)
            for block, b in ((first, 0), (third, 2))
        )
        for (span, left), (span, right) in zip(*pair):
            ready[j, span, :] = (left * right).astype(BF16)
        ready[j, rows : 2 * rows, :] = kept[:, lanes]
        tails = [
            first[rows - ROWS :, lanes].astype(F32)[-edge:],
            rims[1, :, lanes].astype(F32)[-edge:],
            third[rows - ROWS :, lanes].astype(F32)[-edge:],
            first[:ROWS, lanes].astype(F32)[:edge],
            rims[0, :, lanes].astype(F32)[:edge],
            third[:ROWS, lanes].astype(F32)[:edge],
        ]
        unused = height - 2 * rows - 2 * BRANCHES * edge
        if unused:
            tails.append(jnp.zeros((unused, width), F32))
        ready[j, 2 * rows :, :] = jnp.concatenate(tails, axis=0).astype(BF16)
        copy = pltpu.make_async_copy(ready.at[j], out.at[j], outs.at[j])
        copy.start()
        sent.append(copy)
    for copy in sent:
        copy.wait()


def signals_of(branches, taps, filt, parts):
    rows, channels = filt.shape
    width = channels // parts
    height = 2 * rows - (-2 * BRANCHES * (taps.shape[1] - 1) // ROWS) * ROWS
    return pl.pallas_call(
        product_kernel,
        in_specs=[HBM] * 3,
        out_specs=HBM,
        out_shape=jax.ShapeDtypeStruct((parts, height, width), BF16),
        scratch_shapes=[
            pltpu.VMEM(taps.shape, F32),
            pltpu.VMEM((3, rows, channels), BF16),
            pltpu.VMEM((2, ROWS, channels), BF16),
            pltpu.VMEM((parts, height, width), BF16),
            pltpu.VMEM((2, 2, rows + ROWS, width), F32),
            pltpu.SemaphoreType.DMA((3,)),
            pltpu.SemaphoreType.DMA((3,)),
            pltpu.SemaphoreType.DMA((parts,)),
        ],
        compiler_params=pltpu.CompilerParams(vmem_limit_bytes=62 << 20),
        cost_estimate=cost(40 * rows * channels, 10 * rows * channels),
        name="product",
    )(taps, branches, filt)


def unrolled(blocks):
    return 4 if blocks <= 8 else 1


def chunk_of(index, offset=0):
    return pl.ds(pl.multiple_of(offset + index * ROWS, ROWS), ROWS)


def column(twist, rows, index, width):
    return jnp.broadcast_to(twist[rows, index : index + 1], (ROWS, width))


def first_rows(signals, taps, length):
    edge = taps.shape[1] - 1
    rims = signals[:, 2 * length :, :].astype(F32)
    result = []
    for branch in range(BRANCHES):
        before, after = (
            [rims[:, (side * BRANCHES + branch) * edge + i, :] for i in range(edge)]
            for side in (0, 1)
        )
        zero = jnp.zeros_like(before[0][:1])
        rows = [jnp.concatenate([zero, row[:-1]], axis=0) for row in before] + after
        smooth = []
        for i in range(edge):
            total = None
            for tap in range(edge + 1):
                term = rows[edge + i - tap] * taps[branch, tap : tap + 1, :]
                total = term if total is None else total + term
            smooth.append(total)
        result.append(smooth)
    return result


def replaced(tile, rows):
    ids = lax.broadcasted_iota(jnp.int32, tile.shape, 0)
    for i, row in enumerate(rows):
        tile = jnp.where(ids == i, jnp.broadcast_to(row, tile.shape), tile)
    return tile


def transform_kernel(matrix, twist, taps, signals, turned, product, gates, waves):
    blocks, length, width = product.shape
    pairs = blocks // 2

    smooth = first_rows(signals, taps, length)
    for b in range(blocks):
        product[b, ROWS:, :] = signals[b, ROWS:length, :]
        heads = [smooth[0][i][b : b + 1] * smooth[2][i][b : b + 1] for i in range(len(smooth[0]))]
        product[b, :ROWS, :] = replaced(signals[b, :ROWS, :].astype(F32), heads).astype(BF16)
        gains = [smooth[1][i][b : b + 1] for i in range(len(smooth[1]))]
        gates[b] = replaced(jnp.ones((ROWS, width), F32), gains)

    def forward(index, carry):
        rows, low = chunk_of(index), chunk_of(index, length)
        turns = [
            (column(twist, rows, k, width), column(twist, rows, blocks + k, width))
            for k in range(blocks)
        ]
        for side in (0, 1):
            lanes = slice(side * width, (side + 1) * width)
            if side == 0:
                values = [product[b, rows, :].astype(F32) for b in range(blocks)]
            else:
                values = [signals[b, low, :].astype(F32) for b in range(blocks)]
            spectra = across_blocks(values)
            waves[0, rows, lanes] = spectra[0][0].astype(BF16)
            for k in range(1, blocks + 1):
                real, imag = spectra[k]
                cosine, sine = turns[k - 1]
                if imag is None:
                    waves[k, rows, lanes] = (real * cosine).astype(BF16)
                    waves[k, low, lanes] = (-real * sine).astype(BF16)
                else:
                    waves[k, rows, lanes] = (real * cosine + imag * sine).astype(BF16)
                    waves[k, low, lanes] = (imag * cosine - real * sine).astype(BF16)
        return carry

    lax.fori_loop(0, length // ROWS, forward, 0, unroll=unrolled(blocks))

    def multiplied(spectrum):
        real, imag = spectrum[:length], spectrum[length:]
        a_real, a_imag = real[:, :width], imag[:, :width]
        b_real, b_imag = real[:, width:], imag[:, width:]
        return jnp.concatenate(
            [
                (a_real * b_real - a_imag * b_imag).astype(BF16),
                (-(a_real * b_imag + a_imag * b_real)).astype(BF16),
            ],
            axis=0,
        )

    def dot(left, right):
        return jnp.dot(left, right, preferred_element_type=F32)

    base = multiplied(dot(matrix[:, :length], waves[0, :length, :]))
    turned[pairs, :length, :width] = dot(matrix[:length, :], base)

    def one_pair(pair):
        left = multiplied(dot(matrix[...], waves[2 * pair + 1]))
        right = multiplied(dot(matrix[...], waves[2 * pair + 2]))
        turned[pair] = dot(matrix[...], jnp.concatenate([left, right], axis=1))

    if pairs <= 4:
        for pair in range(pairs):
            one_pair(pair)
    else:
        lax.fori_loop(0, pairs, lambda pair, carry: (one_pair(pair), carry)[1], 0)


def back_kernel(twist, gain, gates, turned, product, *outs):
    blocks, length, width = product.shape
    full, pairs = 2 * blocks * length, blocks // 2
    skip = jnp.broadcast_to(gain[...], (ROWS, width))

    def backward(out, start, index, carry):
        rows, low = chunk_of(index, start), chunk_of(index, length + start)
        parts = []
        for k in range(1, blocks + 1):
            pair, side = (k - 1) // 2, (k - 1) % 2
            lanes = slice(side * width, (side + 1) * width)
            real, minus = turned[pair, rows, lanes], turned[pair, low, lanes]
            cosine = column(twist, rows, 2 * blocks + k - 1, width)
            sine = column(twist, rows, 3 * blocks + k - 1, width)
            turned_real = real * cosine + minus * sine
            parts.append((turned_real, None if k == blocks else real * sine - minus * cosine))
        first = turned[pairs, rows, :width] * np.float32(1.0 / full)
        for b, value in enumerate(back_to_blocks(first, parts)):
            direct = skip * product[b, rows, :].astype(F32)
            out[b, chunk_of(index), :] = (value + direct).astype(BF16)
        return carry

    start = 0
    for out in outs:
        body = functools.partial(backward, out, start)
        lax.fori_loop(0, out.shape[1] // ROWS, body, 0, unroll=unrolled(blocks))
        start += out.shape[1]
    for b in range(blocks):
        outs[0][b, :ROWS, :] = (outs[0][b, :ROWS, :].astype(F32) * gates[b]).astype(BF16)


def weight_copies(weight, held, sems, block):
    depth, columns = held.shape
    span = pl.ds(pl.multiple_of(block * columns, columns), columns)
    step = depth // PIECES
    pieces = [pl.ds(i * step, step) for i in range(PIECES)]
    return [
        pltpu.make_async_copy(weight.at[rows, span], held.at[rows, :], sems.at[i])
        for i, rows in enumerate(pieces)
    ]


def start_all(copies):
    for copy in copies:
        copy.start()


def project_into(outs, gated, weight, copies, total):
    depth, columns = weight.shape
    group = PIECES // STEPS
    for step in range(STEPS):
        for copy in copies[step * group : (step + 1) * group]:
            copy.wait()
        rows = slice(step * depth // STEPS, (step + 1) * depth // STEPS)
        for start in range(0, columns, TILE):
            span = slice(start, start + TILE)
            value = jnp.dot(gated[:, rows], weight[rows, span], preferred_element_type=F32)
            if step:
                value = total[:, span] + value
            if step < STEPS - 1:
                total[:, span] = value
            else:
                index, offset = divmod(start, columns // len(outs))
                out = outs[index]
                out[:, offset : offset + TILE] = value.astype(out.dtype)


def gated_rows(start, mixed, branch, taps, gated, padded):
    parts, rows, width = mixed.shape
    for j in range(parts):
        lanes = slice(j * width, (j + 1) * width)
        strips = smoothed(branch, lanes, tap_rows(taps, 1, lanes), padded.at[j % 2], rows, start)
        for span, second in strips:
            value = mixed[j, span, :].astype(F32)
            done = second * value
            if start == 0 and span.start == 0:
                ids = lax.broadcasted_iota(jnp.int32, done.shape, 0)
                done = jnp.where(ids < taps.shape[1] - 1, value, done)
            gated[span, lanes] = done.astype(BF16)


def gate_kernel(start, place, mixed, branch, taps, weight, gated, part, padded, held, sems, total):
    copies = weight_copies(weight, held.at[0], sems.at[0], place[0] ^ 3)
    start_all(copies)
    gated_rows(start, mixed, branch, taps, gated, padded)
    project_into([part], gated, held.at[0], copies, total)


def own_kernel(place, gated, weight, own, held, sems, total):
    copies = weight_copies(weight, held.at[0], sems.at[0], place[0] ^ 2)
    start_all(copies)
    project_into([own], gated, held.at[0], copies, total)


def near_kernel(place, first, second, weight, *rest):
    *parts, own, held, sems, total, gated = rest
    sets = [weight_copies(weight, held.at[i], sems.at[i], place[0] ^ (1 - i)) for i in (0, 1)]
    start_all(sets[0])
    start_all(sets[1])
    rows = first.shape[0]
    gated[:rows, :] = first[...]
    gated[rows:, :] = second[...]
    project_into(parts, gated, held.at[0], sets[0], total)
    project_into([own], gated, held.at[1], sets[1], total)


def shards(branches, short_filter, long_filter, skip_gain, out_weight):
    seq_count, mp_count = lax.axis_size("seq"), lax.axis_size("mp")
    tokens, channels = long_filter.shape
    width = channels // seq_count
    features = out_weight.shape[1] // mp_count
    me, place = lax.axis_index("mp").reshape(1), lax.axis_index("seq")
    params = pltpu.CompilerParams(vmem_limit_bytes=50 << 20)
    small = pltpu.CompilerParams(vmem_limit_bytes=24 << 20)

    def exchanged(value, bit):
        return lax.ppermute(value, "mp", [(m, m ^ bit) for m in range(mp_count)])

    def across(value):
        return lax.all_to_all(value, "seq", 0, 0, tiled=True)

    def shape(dtype, rows):
        return jax.ShapeDtypeStruct((rows, features), dtype)

    taps = jnp.transpose(short_filter, (0, 2, 1))
    signals = across(signals_of(branches, taps, long_filter, seq_count))

    mine = place * width
    gain = lax.dynamic_slice(skip_gain, (mine,), (width,)).reshape(1, width)
    my_taps = lax.dynamic_slice_in_dim(taps, mine, width, 2)
    matrix, twist = (jnp.asarray(t) for t in transform_tables(tokens, 2 * seq_count))
    turned, product, gates = pl.pallas_call(
        transform_kernel,
        in_specs=[VMEM] * 4,
        out_specs=[VMEM] * 3,
        out_shape=[
            jax.ShapeDtypeStruct((seq_count // 2 + 1, 2 * tokens, 2 * width), F32),
            jax.ShapeDtypeStruct((seq_count, tokens, width), BF16),
            jax.ShapeDtypeStruct((seq_count, ROWS, width), F32),
        ],
        scratch_shapes=[pltpu.VMEM((seq_count + 1, 2 * tokens, 2 * width), BF16)],
        compiler_params=small,
        cost_estimate=cost(seq_count * 12 * (2 * tokens) ** 2 * width, 6 << 20),
        name="transform",
    )(matrix, twist, my_taps, signals)
    counts = (tokens * 176 // 256, tokens * 80 // 256)
    mixed = pl.pallas_call(
        back_kernel,
        in_specs=[VMEM] * 5,
        out_specs=[VMEM] * len(counts),
        out_shape=[jax.ShapeDtypeStruct((seq_count, count, width), BF16) for count in counts],
        compiler_params=small,
        cost_estimate=cost(200 * tokens * channels, 5 << 20),
        name="back",
    )(twist, gain, gates, turned, product)

    flops, moved = 2 * tokens * channels * features, 2 * channels * features
    held = pltpu.VMEM((2, channels, features), BF16)
    sems = pltpu.SemaphoreType.DMA((2, PIECES))
    gated, far = [], []
    start = 0
    for step, (value, count) in enumerate(zip(mixed, counts)):
        padded = pltpu.VMEM((2, count + ROWS, width), F32)
        total = pltpu.VMEM((count, features), F32)
        if step:
            value, sent = lax.optimization_barrier((value, sent))
        value = across(value)
        ready, part = pl.pallas_call(
            functools.partial(gate_kernel, start),
            in_specs=[SMEM] + [VMEM] * 3 + [HBM],
            out_specs=[VMEM] * 2,
            out_shape=[jax.ShapeDtypeStruct((count, channels), BF16), shape(BF16, count)],
            scratch_shapes=[padded, held, sems, total],
            compiler_params=params,
            cost_estimate=cost(1, 1),
            name="gate",
        )(me, value, branches[1], taps, out_weight)
        other = exchanged(part, 1)
        own = pl.pallas_call(
            own_kernel,
            in_specs=[SMEM, VMEM, HBM],
            out_specs=VMEM,
            out_shape=shape(F32, count),
            scratch_shapes=[held, sems, total],
            compiler_params=params,
            cost_estimate=cost(1, 1),
            name="own",
        )(me, ready, out_weight)
        if step:
            own, far[0] = lax.optimization_barrier((own, far[0]))
        sent = (own + other.astype(F32)).astype(BF16)
        gated.append(ready)
        far.append(exchanged(sent, 2))
        start += count
    gated[0], gated[1], sent = lax.optimization_barrier((gated[0], gated[1], sent))
    pieces = 4
    *near_part, near_own = pl.pallas_call(
        near_kernel,
        in_specs=[SMEM, VMEM, VMEM, HBM],
        out_specs=[VMEM] * (pieces + 1),
        out_shape=[jax.ShapeDtypeStruct((tokens, features // pieces), BF16)] * pieces
        + [shape(F32, tokens)],
        scratch_shapes=[
            held,
            sems,
            pltpu.VMEM((tokens, features), F32),
            pltpu.VMEM((tokens, channels), BF16),
        ],
        compiler_params=params,
        cost_estimate=cost(1, 1),
        name="near",
    )(me, *gated, out_weight)
    near_part = jnp.concatenate([exchanged(part, 1) for part in near_part], axis=1)
    near = near_own + near_part.astype(F32)
    return (near + jnp.concatenate(far, axis=0).astype(F32)).astype(BF16)


def solution(mesh):
    return jax.shard_map(
        shards,
        mesh=mesh,
        in_specs=(
            P(None, "seq", "mp"),
            P(None, "mp", None),
            P("seq", "mp"),
            P("mp"),
            P("mp", None),
        ),
        out_specs=P("seq", "mp"),
        check_vma=False,
    )
```

```python
import functools
import math

import jax
import jax.numpy as jnp
import numpy as np
from jax import lax
from jax.experimental import pallas as pl
from jax.experimental.pallas import tpu as pltpu
from jax.sharding import PartitionSpec as P

ROWS = 16
F32 = jnp.float32
BF16 = jnp.bfloat16


def transform_tables(length, radix):
    ids = np.arange(length)
    angle = 2.0 * math.pi * np.mod(np.outer(ids, ids), length) / length
    cosine, sine = np.cos(angle), np.sin(angle)
    matrix = np.block([[cosine, sine], [-sine, cosine]]).astype(jnp.bfloat16)
    full = length * radix
    turn = 2.0 * math.pi * np.outer(ids, np.arange(1, radix // 2 + 1)) / full
    scale = np.where(np.arange(1, radix // 2 + 1) == radix // 2, 1.0, 2.0) / full
    columns = [np.cos(turn), np.sin(turn), np.cos(turn) * scale, np.sin(turn) * scale]
    return matrix, np.concatenate(columns, axis=1).astype(np.float32)


def axpy(total, factor, value):
    if abs(factor) < 1e-9:
        return total
    if abs(factor - 1.0) < 1e-9:
        return value if total is None else total + value
    if abs(factor + 1.0) < 1e-9:
        return -value if total is None else total - value
    term = value * np.float32(factor)
    return term if total is None else total + term


def wave(step, radix):
    angle = 2.0 * math.pi * (step % radix) / radix
    return math.cos(angle), math.sin(angle)


def combined(signs, terms):
    total = None
    for sign, term in zip(signs, terms):
        if term is not None:
            total = axpy(total, sign, term)
    return total


def across_blocks(values):
    count = len(values)
    radix, half = 2 * count, count // 2
    sums = {n: values[n] + values[count - n] for n in range(1, half)}
    diffs = {n: values[n] - values[count - n] for n in range(1, half)}
    result = [None] * (count + 1)
    for k in range(half + 1):
        in_cos, in_sin = (sums, diffs) if k % 2 == 0 else (diffs, sums)
        real = [axpy(values[0], wave(half * k, radix)[0], values[half]), None]
        imag = [axpy(None, -wave(half * k, radix)[1], values[half]), None]
        for n in range(1, half):
            cosine, sine = wave(n * k, radix)
            real[n % 2] = axpy(real[n % 2], cosine, in_cos[n])
            imag[n % 2] = axpy(imag[n % 2], -sine, in_sin[n])
        result[k] = (combined([1, 1], real), combined([1, 1], imag))
        if k < half:
            result[count - k] = (combined([1, -1], real), combined([-1, 1], imag))
    return result


def back_to_blocks(first, parts):
    count = len(parts)
    radix, half = 2 * count, count // 2
    result = [None] * count
    for n in range(half + 1):
        even_cos, even_sin, odd_cos, odd_sin = first, None, None, None
        for k in range(1, count + 1):
            real, imag = parts[k - 1]
            cosine, sine = wave(n * k, radix)
            if k % 2 == 0:
                even_cos = axpy(even_cos, cosine, real)
                if imag is not None:
                    even_sin = axpy(even_sin, -sine, imag)
            else:
                odd_cos = axpy(odd_cos, cosine, real)
                odd_sin = axpy(odd_sin, -sine, imag)

        terms = (even_cos, even_sin, odd_cos, odd_sin)
        result[n] = combined((1, 1, 1, 1), terms)
        if 0 < n < half:
            result[count - n] = combined((1, -1, -1, 1), terms)
    return result


VMEM = pl.BlockSpec(memory_space=pltpu.VMEM)
SMEM = pl.BlockSpec(memory_space=pltpu.SMEM)
HBM = pl.BlockSpec(memory_space=pltpu.HBM)
TILE = 512
PIECES = 4
STEPS = 4
BRANCHES = 3


def cost(flops, moved):
    return pl.CostEstimate(flops=int(flops), bytes_accessed=int(moved), transcendentals=0)


def smoothed(block, lanes, taps, padded, rows, start=0):
    if start == 0:
        padded[:ROWS, :] = jnp.zeros((ROWS, padded.shape[1]), F32)
    else:
        padded[:ROWS, :] = block[start - ROWS : start, lanes].astype(F32)
    strip = next(n for n in (64, 32, 16) if rows % n == 0)
    for begin in range(0, rows, strip):
        value = block[start + begin : start + begin + strip, lanes].astype(F32)
        padded[ROWS + begin : ROWS + begin + strip, :] = value
    for begin in range(0, rows, strip):
        total = None
        for tap in range(len(taps)):
            first = ROWS - tap + begin
            term = padded[first : first + strip, :] * taps[tap]
            total = term if total is None else total + term
        yield slice(begin, begin + strip), total


def tap_rows(taps, branch, lanes):
    return [taps[branch, tap : tap + 1, lanes] for tap in range(taps.shape[1])]


def product_kernel(all_taps, branches, filt, out, taps, held, rims, ready, padded, ins, ends, outs):
    parts, height, width = out.shape
    rows, edge = filt.shape[0], taps.shape[1] - 1
    copies = [pltpu.make_async_copy(all_taps, taps, ends.at[2])]
    for side in (0, 1):
        source = branches.at[1, pl.ds(side * (rows - ROWS), ROWS), :]
        copies.append(pltpu.make_async_copy(source, rims.at[side], ends.at[side]))
    for i, source in enumerate((branches.at[0], branches.at[2], filt)):
        copies.append(pltpu.make_async_copy(source, held.at[i], ins.at[i]))
    for copy in copies:
        copy.start()
    for copy in copies:
        copy.wait()
    first, third, kept = (held.at[i] for i in range(3))
    sent = []
    for j in range(parts):
        lanes = slice(j * width, (j + 1) * width)
        pair = (
            smoothed(block, lanes, tap_rows(taps, b, lanes), padded.at[j % 2, b // 2], rows)
            for block, b in ((first, 0), (third, 2))
        )
        for (span, left), (span, right) in zip(*pair):
            ready[j, span, :] = (left * right).astype(BF16)
        ready[j, rows : 2 * rows, :] = kept[:, lanes]
        tails = [
            first[rows - ROWS :, lanes].astype(F32)[-edge:],
            rims[1, :, lanes].astype(F32)[-edge:],
            third[rows - ROWS :, lanes].astype(F32)[-edge:],
            first[:ROWS, lanes].astype(F32)[:edge],
            rims[0, :, lanes].astype(F32)[:edge],
            third[:ROWS, lanes].astype(F32)[:edge],
        ]
        unused = height - 2 * rows - 2 * BRANCHES * edge
        if unused:
            tails.append(jnp.zeros((unused, width), F32))
        ready[j, 2 * rows :, :] = jnp.concatenate(tails, axis=0).astype(BF16)
        copy = pltpu.make_async_copy(ready.at[j], out.at[j], outs.at[j])
        copy.start()
        sent.append(copy)
    for copy in sent:
        copy.wait()


def signals_of(branches, taps, filt, parts):
    rows, channels = filt.shape
    width = channels // parts
    height = 2 * rows - (-2 * BRANCHES * (taps.shape[1] - 1) // ROWS) * ROWS
    return pl.pallas_call(
        product_kernel,
        in_specs=[HBM] * 3,
        out_specs=HBM,
        out_shape=jax.ShapeDtypeStruct((parts, height, width), BF16),
        scratch_shapes=[
            pltpu.VMEM(taps.shape, F32),
            pltpu.VMEM((3, rows, channels), BF16),
            pltpu.VMEM((2, ROWS, channels), BF16),
            pltpu.VMEM((parts, height, width), BF16),
            pltpu.VMEM((2, 2, rows + ROWS, width), F32),
            pltpu.SemaphoreType.DMA((3,)),
            pltpu.SemaphoreType.DMA((3,)),
            pltpu.SemaphoreType.DMA((parts,)),
        ],
        compiler_params=pltpu.CompilerParams(vmem_limit_bytes=62 << 20),
        cost_estimate=cost(40 * rows * channels, 10 * rows * channels),
        name="product",
    )(taps, branches, filt)


def unrolled(blocks):
    return 4 if blocks <= 8 else 1


def chunk_of(index, offset=0):
    return pl.ds(pl.multiple_of(offset + index * ROWS, ROWS), ROWS)


def column(twist, rows, index, width):
    return jnp.broadcast_to(twist[rows, index : index + 1], (ROWS, width))


def first_rows(signals, taps, length):
    edge = taps.shape[1] - 1
    rims = signals[:, 2 * length :, :].astype(F32)
    result = []
    for branch in range(BRANCHES):
        before, after = (
            [rims[:, (side * BRANCHES + branch) * edge + i, :] for i in range(edge)]
            for side in (0, 1)
        )
        zero = jnp.zeros_like(before[0][:1])
        rows = [jnp.concatenate([zero, row[:-1]], axis=0) for row in before] + after
        smooth = []
        for i in range(edge):
            total = None
            for tap in range(edge + 1):
                term = rows[edge + i - tap] * taps[branch, tap : tap + 1, :]
                total = term if total is None else total + term
            smooth.append(total)
        result.append(smooth)
    return result


def replaced(tile, rows):
    ids = lax.broadcasted_iota(jnp.int32, tile.shape, 0)
    for i, row in enumerate(rows):
        tile = jnp.where(ids == i, jnp.broadcast_to(row, tile.shape), tile)
    return tile


def transform_kernel(matrix, twist, taps, signals, turned, product, gates, waves):
    blocks, length, width = product.shape
    pairs = blocks // 2

    smooth = first_rows(signals, taps, length)
    for b in range(blocks):
        product[b, ROWS:, :] = signals[b, ROWS:length, :]
        heads = [smooth[0][i][b : b + 1] * smooth[2][i][b : b + 1] for i in range(len(smooth[0]))]
        product[b, :ROWS, :] = replaced(signals[b, :ROWS, :].astype(F32), heads).astype(BF16)
        gains = [smooth[1][i][b : b + 1] for i in range(len(smooth[1]))]
        gates[b] = replaced(jnp.ones((ROWS, width), F32), gains)

    def forward(index, carry):
        rows, low = chunk_of(index), chunk_of(index, length)
        turns = [
            (column(twist, rows, k, width), column(twist, rows, blocks + k, width))
            for k in range(blocks)
        ]
        for side in (0, 1):
            lanes = slice(side * width, (side + 1) * width)
            if side == 0:
                values = [product[b, rows, :].astype(F32) for b in range(blocks)]
            else:
                values = [signals[b, low, :].astype(F32) for b in range(blocks)]
            spectra = across_blocks(values)
            waves[0, rows, lanes] = spectra[0][0].astype(BF16)
            for k in range(1, blocks + 1):
                real, imag = spectra[k]
                cosine, sine = turns[k - 1]
                if imag is None:
                    waves[k, rows, lanes] = (real * cosine).astype(BF16)
                    waves[k, low, lanes] = (-real * sine).astype(BF16)
                else:
                    waves[k, rows, lanes] = (real * cosine + imag * sine).astype(BF16)
                    waves[k, low, lanes] = (imag * cosine - real * sine).astype(BF16)
        return carry

    lax.fori_loop(0, length // ROWS, forward, 0, unroll=unrolled(blocks))

    def multiplied(spectrum):
        real, imag = spectrum[:length], spectrum[length:]
        a_real, a_imag = real[:, :width], imag[:, :width]
        b_real, b_imag = real[:, width:], imag[:, width:]
        return jnp.concatenate(
            [
                (a_real * b_real - a_imag * b_imag).astype(BF16),
                (-(a_real * b_imag + a_imag * b_real)).astype(BF16),
            ],
            axis=0,
        )

    def dot(left, right):
        return jnp.dot(left, right, preferred_element_type=F32)

    base = multiplied(dot(matrix[:, :length], waves[0, :length, :]))
    turned[pairs, :length, :width] = dot(matrix[:length, :], base)

    def one_pair(pair):
        left = multiplied(dot(matrix[...], waves[2 * pair + 1]))
        right = multiplied(dot(matrix[...], waves[2 * pair + 2]))
        turned[pair] = dot(matrix[...], jnp.concatenate([left, right], axis=1))

    if pairs <= 4:
        for pair in range(pairs):
            one_pair(pair)
    else:
        lax.fori_loop(0, pairs, lambda pair, carry: (one_pair(pair), carry)[1], 0)


def back_kernel(twist, gain, gates, turned, product, *outs):
    blocks, length, width = product.shape
    full, pairs = 2 * blocks * length, blocks // 2
    skip = jnp.broadcast_to(gain[...], (ROWS, width))

    def backward(out, start, index, carry):
        rows, low = chunk_of(index, start), chunk_of(index, length + start)
        parts = []
        for k in range(1, blocks + 1):
            pair, side = (k - 1) // 2, (k - 1) % 2
            lanes = slice(side * width, (side + 1) * width)
            real, minus = turned[pair, rows, lanes], turned[pair, low, lanes]
            cosine = column(twist, rows, 2 * blocks + k - 1, width)
            sine = column(twist, rows, 3 * blocks + k - 1, width)
            turned_real = real * cosine + minus * sine
            parts.append((turned_real, None if k == blocks else real * sine - minus * cosine))
        first = turned[pairs, rows, :width] * np.float32(1.0 / full)
        for b, value in enumerate(back_to_blocks(first, parts)):
            direct = skip * product[b, rows, :].astype(F32)
            out[b, chunk_of(index), :] = (value + direct).astype(BF16)
        return carry

    start = 0
    for out in outs:
        body = functools.partial(backward, out, start)
        lax.fori_loop(0, out.shape[1] // ROWS, body, 0, unroll=unrolled(blocks))
        start += out.shape[1]
    for b in range(blocks):
        outs[0][b, :ROWS, :] = (outs[0][b, :ROWS, :].astype(F32) * gates[b]).astype(BF16)


def weight_copies(weight, held, sems, block):
    depth, columns = held.shape
    span = pl.ds(pl.multiple_of(block * columns, columns), columns)
    step = depth // PIECES
    pieces = [pl.ds(i * step, step) for i in range(PIECES)]
    return [
        pltpu.make_async_copy(weight.at[rows, span], held.at[rows, :], sems.at[i])
        for i, rows in enumerate(pieces)
    ]


def start_all(copies):
    for copy in copies:
        copy.start()


def project_into(outs, gated, weight, copies, total):
    depth, columns = weight.shape
    group = PIECES // STEPS
    for step in range(STEPS):
        for copy in copies[step * group : (step + 1) * group]:
            copy.wait()
        rows = slice(step * depth // STEPS, (step + 1) * depth // STEPS)
        for start in range(0, columns, TILE):
            span = slice(start, start + TILE)
            value = jnp.dot(gated[:, rows], weight[rows, span], preferred_element_type=F32)
            if step:
                value = total[:, span] + value
            if step < STEPS - 1:
                total[:, span] = value
            else:
                index, offset = divmod(start, columns // len(outs))
                out = outs[index]
                out[:, offset : offset + TILE] = value.astype(out.dtype)


def gated_rows(start, mixed, branch, taps, gated, padded):
    parts, rows, width = mixed.shape
    for j in range(parts):
        lanes = slice(j * width, (j + 1) * width)
        strips = smoothed(branch, lanes, tap_rows(taps, 1, lanes), padded.at[j % 2], rows, start)
        for span, second in strips:
            value = mixed[j, span, :].astype(F32)
            done = second * value
            if start == 0 and span.start == 0:
                ids = lax.broadcasted_iota(jnp.int32, done.shape, 0)
                done = jnp.where(ids < taps.shape[1] - 1, value, done)
            gated[span, lanes] = done.astype(BF16)


def gate_kernel(start, place, mixed, branch, taps, weight, gated, part, padded, held, sems, total):
    copies = weight_copies(weight, held.at[0], sems.at[0], place[0] ^ 3)
    start_all(copies)
    gated_rows(start, mixed, branch, taps, gated, padded)
    project_into([part], gated, held.at[0], copies, total)


def own_kernel(place, gated, weight, own, held, sems, total):
    copies = weight_copies(weight, held.at[0], sems.at[0], place[0] ^ 2)
    start_all(copies)
    project_into([own], gated, held.at[0], copies, total)


def near_kernel(place, first, second, weight, *rest):
    *parts, own, held, sems, total, gated = rest
    sets = [weight_copies(weight, held.at[i], sems.at[i], place[0] ^ (1 - i)) for i in (0, 1)]
    start_all(sets[0])
    start_all(sets[1])
    rows = first.shape[0]
    gated[:rows, :] = first[...]
    gated[rows:, :] = second[...]
    project_into(parts, gated, held.at[0], sets[0], total)
    project_into([own], gated, held.at[1], sets[1], total)


def shards(branches, short_filter, long_filter, skip_gain, out_weight):
    seq_count, mp_count = lax.axis_size("seq"), lax.axis_size("mp")
    tokens, channels = long_filter.shape
    width = channels // seq_count
    features = out_weight.shape[1] // mp_count
    me, place = lax.axis_index("mp").reshape(1), lax.axis_index("seq")
    params = pltpu.CompilerParams(vmem_limit_bytes=50 << 20)
    small = pltpu.CompilerParams(vmem_limit_bytes=24 << 20)

    def exchanged(value, bit):
        return lax.ppermute(value, "mp", [(m, m ^ bit) for m in range(mp_count)])

    def across(value):
        return lax.all_to_all(value, "seq", 0, 0, tiled=True)

    def shape(dtype, rows):
        return jax.ShapeDtypeStruct((rows, features), dtype)

    taps = jnp.transpose(short_filter, (0, 2, 1))
    signals = across(signals_of(branches, taps, long_filter, seq_count))

    mine = place * width
    gain = lax.dynamic_slice(skip_gain, (mine,), (width,)).reshape(1, width)
    my_taps = lax.dynamic_slice_in_dim(taps, mine, width, 2)
    matrix, twist = (jnp.asarray(t) for t in transform_tables(tokens, 2 * seq_count))
    turned, product, gates = pl.pallas_call(
        transform_kernel,
        in_specs=[VMEM] * 4,
        out_specs=[VMEM] * 3,
        out_shape=[
            jax.ShapeDtypeStruct((seq_count // 2 + 1, 2 * tokens, 2 * width), F32),
            jax.ShapeDtypeStruct((seq_count, tokens, width), BF16),
            jax.ShapeDtypeStruct((seq_count, ROWS, width), F32),
        ],
        scratch_shapes=[pltpu.VMEM((seq_count + 1, 2 * tokens, 2 * width), BF16)],
        compiler_params=small,
        cost_estimate=cost(seq_count * 12 * (2 * tokens) ** 2 * width, 6 << 20),
        name="transform",
    )(matrix, twist, my_taps, signals)
    counts = (tokens * 176 // 256, tokens * 80 // 256)
    mixed = pl.pallas_call(
        back_kernel,
        in_specs=[VMEM] * 5,
        out_specs=[VMEM] * len(counts),
        out_shape=[jax.ShapeDtypeStruct((seq_count, count, width), BF16) for count in counts],
        compiler_params=small,
        cost_estimate=cost(200 * tokens * channels, 5 << 20),
        name="back",
    )(twist, gain, gates, turned, product)

    flops, moved = 2 * tokens * channels * features, 2 * channels * features
    held = pltpu.VMEM((2, channels, features), BF16)
    sems = pltpu.SemaphoreType.DMA((2, PIECES))
    gated, far = [], []
    start = 0
    for step, (value, count) in enumerate(zip(mixed, counts)):
        padded = pltpu.VMEM((2, count + ROWS, width), F32)
        total = pltpu.VMEM((count, features), F32)
        if step:
            value, sent = lax.optimization_barrier((value, sent))
        value = across(value)
        ready, part = pl.pallas_call(
            functools.partial(gate_kernel, start),
            in_specs=[SMEM] + [VMEM] * 3 + [HBM],
            out_specs=[VMEM] * 2,
            out_shape=[jax.ShapeDtypeStruct((count, channels), BF16), shape(BF16, count)],
            scratch_shapes=[padded, held, sems, total],
            compiler_params=params,
            cost_estimate=cost(1, 1),
            name="gate",
        )(me, value, branches[1], taps, out_weight)
        other = exchanged(part, 1)
        own = pl.pallas_call(
            own_kernel,
            in_specs=[SMEM, VMEM, HBM],
            out_specs=VMEM,
            out_shape=shape(F32, count),
            scratch_shapes=[held, sems, total],
            compiler_params=params,
            cost_estimate=cost(1, 1),
            name="own",
        )(me, ready, out_weight)
        if step:
            own, far[0] = lax.optimization_barrier((own, far[0]))
        sent = (own + other.astype(F32)).astype(BF16)
        gated.append(ready)
        far.append(exchanged(sent, 2))
        start += count
    gated[0], gated[1], sent = lax.optimization_barrier((gated[0], gated[1], sent))
    pieces = 4
    *near_part, near_own = pl.pallas_call(
        near_kernel,
        in_specs=[SMEM, VMEM, VMEM, HBM],
        out_specs=[VMEM] * (pieces + 1),
        out_shape=[jax.ShapeDtypeStruct((tokens, features // pieces), BF16)] * pieces
        + [shape(F32, tokens)],
        scratch_shapes=[
            held,
            sems,
            pltpu.VMEM((tokens, features), F32),
            pltpu.VMEM((tokens, channels), BF16),
        ],
        compiler_params=params,
        cost_estimate=cost(1, 1),
        name="near",
    )(me, *gated, out_weight)
    near_part = jnp.concatenate([exchanged(part, 1) for part in near_part], axis=1)
    near = near_own + near_part.astype(F32)
    return (near + jnp.concatenate(far, axis=0).astype(F32)).astype(BF16)


def solution(mesh):
    return jax.shard_map(
        shards,
        mesh=mesh,
        in_specs=(
            P(None, "seq", "mp"),
            P(None, "mp", None),
            P("seq", "mp"),
            P("mp"),
            P("mp", None),
        ),
        out_specs=P("seq", "mp"),
        check_vma=False,
    )
```

```python
import functools
import math

import jax
import jax.numpy as jnp
import numpy as np
from jax import lax
from jax.experimental import pallas as pl
from jax.experimental.pallas import tpu as pltpu
from jax.sharding import PartitionSpec as P

ROWS = 16
F32 = jnp.float32
BF16 = jnp.bfloat16


def transform_tables(length, radix):
    ids = np.arange(length)
    angle = 2.0 * math.pi * np.mod(np.outer(ids, ids), length) / length
    cosine, sine = np.cos(angle), np.sin(angle)
    matrix = np.block([[cosine, sine], [-sine, cosine]]).astype(jnp.bfloat16)
    full = length * radix
    turn = 2.0 * math.pi * np.outer(ids, np.arange(1, radix // 2 + 1)) / full
    scale = np.where(np.arange(1, radix // 2 + 1) == radix // 2, 1.0, 2.0) / full
    columns = [np.cos(turn), np.sin(turn), np.cos(turn) * scale, np.sin(turn) * scale]
    return matrix, np.concatenate(columns, axis=1).astype(np.float32)


def axpy(total, factor, value):
    if abs(factor) < 1e-9:
        return total
    if abs(factor - 1.0) < 1e-9:
        return value if total is None else total + value
    if abs(factor + 1.0) < 1e-9:
        return -value if total is None else total - value
    term = value * np.float32(factor)
    return term if total is None else total + term


def wave(step, radix):
    angle = 2.0 * math.pi * (step % radix) / radix
    return math.cos(angle), math.sin(angle)


def combined(signs, terms):
    total = None
    for sign, term in zip(signs, terms):
        if term is not None:
            total = axpy(total, sign, term)
    return total


def across_blocks(values):
    count = len(values)
    radix, half = 2 * count, count // 2
    sums = {n: values[n] + values[count - n] for n in range(1, half)}
    diffs = {n: values[n] - values[count - n] for n in range(1, half)}
    result = [None] * (count + 1)
    for k in range(half + 1):
        in_cos, in_sin = (sums, diffs) if k % 2 == 0 else (diffs, sums)
        real = [axpy(values[0], wave(half * k, radix)[0], values[half]), None]
        imag = [axpy(None, -wave(half * k, radix)[1], values[half]), None]
        for n in range(1, half):
            cosine, sine = wave(n * k, radix)
            real[n % 2] = axpy(real[n % 2], cosine, in_cos[n])
            imag[n % 2] = axpy(imag[n % 2], -sine, in_sin[n])
        result[k] = (combined([1, 1], real), combined([1, 1], imag))
        if k < half:
            result[count - k] = (combined([1, -1], real), combined([-1, 1], imag))
    return result


def back_to_blocks(first, parts):
    count = len(parts)
    radix, half = 2 * count, count // 2
    result = [None] * count
    for n in range(half + 1):
        even_cos, even_sin, odd_cos, odd_sin = first, None, None, None
        for k in range(1, count + 1):
            real, imag = parts[k - 1]
            cosine, sine = wave(n * k, radix)
            if k % 2 == 0:
                even_cos = axpy(even_cos, cosine, real)
                if imag is not None:
                    even_sin = axpy(even_sin, -sine, imag)
            else:
                odd_cos = axpy(odd_cos, cosine, real)
                odd_sin = axpy(odd_sin, -sine, imag)

        terms = (even_cos, even_sin, odd_cos, odd_sin)
        result[n] = combined((1, 1, 1, 1), terms)
        if 0 < n < half:
            result[count - n] = combined((1, -1, -1, 1), terms)
    return result


VMEM = pl.BlockSpec(memory_space=pltpu.VMEM)
SMEM = pl.BlockSpec(memory_space=pltpu.SMEM)
HBM = pl.BlockSpec(memory_space=pltpu.HBM)
TILE = 256
PIECES = 4
STEPS = 4
BRANCHES = 3


def cost(flops, moved):
    return pl.CostEstimate(flops=int(flops), bytes_accessed=int(moved), transcendentals=0)


def smoothed(block, lanes, taps, padded, rows, start=0):
    if start == 0:
        padded[:ROWS, :] = jnp.zeros((ROWS, padded.shape[1]), F32)
    else:
        padded[:ROWS, :] = block[start - ROWS : start, lanes].astype(F32)
    strip = next(n for n in (64, 32, 16) if rows % n == 0)
    for begin in range(0, rows, strip):
        value = block[start + begin : start + begin + strip, lanes].astype(F32)
        padded[ROWS + begin : ROWS + begin + strip, :] = value
    for begin in range(0, rows, strip):
        total = None
        for tap in range(len(taps)):
            first = ROWS - tap + begin
            term = padded[first : first + strip, :] * taps[tap]
            total = term if total is None else total + term
        yield slice(begin, begin + strip), total


def tap_rows(taps, branch, lanes):
    return [taps[branch, tap : tap + 1, lanes] for tap in range(taps.shape[1])]


def product_kernel(all_taps, branches, filt, out, taps, held, rims, ready, padded, ins, ends, outs):
    parts, height, width = out.shape
    rows, edge = filt.shape[0], taps.shape[1] - 1
    copies = [pltpu.make_async_copy(all_taps, taps, ends.at[2])]
    for side in (0, 1):
        source = branches.at[1, pl.ds(side * (rows - ROWS), ROWS), :]
        copies.append(pltpu.make_async_copy(source, rims.at[side], ends.at[side]))
    for i, source in enumerate((branches.at[0], branches.at[2], filt)):
        copies.append(pltpu.make_async_copy(source, held.at[i], ins.at[i]))
    for copy in copies:
        copy.start()
    for copy in copies:
        copy.wait()
    first, third, kept = (held.at[i] for i in range(3))
    sent = []
    for j in range(parts):
        lanes = slice(j * width, (j + 1) * width)
        pair = (
            smoothed(block, lanes, tap_rows(taps, b, lanes), padded.at[j % 2, b // 2], rows)
            for block, b in ((first, 0), (third, 2))
        )
        for (span, left), (span, right) in zip(*pair):
            ready[j, span, :] = (left * right).astype(BF16)
        ready[j, rows : 2 * rows, :] = kept[:, lanes]
        tails = [
            first[rows - ROWS :, lanes].astype(F32)[-edge:],
            rims[1, :, lanes].astype(F32)[-edge:],
            third[rows - ROWS :, lanes].astype(F32)[-edge:],
            first[:ROWS, lanes].astype(F32)[:edge],
            rims[0, :, lanes].astype(F32)[:edge],
            third[:ROWS, lanes].astype(F32)[:edge],
        ]
        unused = height - 2 * rows - 2 * BRANCHES * edge
        if unused:
            tails.append(jnp.zeros((unused, width), F32))
        ready[j, 2 * rows :, :] = jnp.concatenate(tails, axis=0).astype(BF16)
        copy = pltpu.make_async_copy(ready.at[j], out.at[j], outs.at[j])
        copy.start()
        sent.append(copy)
    for copy in sent:
        copy.wait()


def signals_of(branches, taps, filt, parts):
    rows, channels = filt.shape
    width = channels // parts
    height = 2 * rows - (-2 * BRANCHES * (taps.shape[1] - 1) // ROWS) * ROWS
    return pl.pallas_call(
        product_kernel,
        in_specs=[HBM] * 3,
        out_specs=HBM,
        out_shape=jax.ShapeDtypeStruct((parts, height, width), BF16),
        scratch_shapes=[
            pltpu.VMEM(taps.shape, F32),
            pltpu.VMEM((3, rows, channels), BF16),
            pltpu.VMEM((2, ROWS, channels), BF16),
            pltpu.VMEM((parts, height, width), BF16),
            pltpu.VMEM((2, 2, rows + ROWS, width), F32),
            pltpu.SemaphoreType.DMA((3,)),
            pltpu.SemaphoreType.DMA((3,)),
            pltpu.SemaphoreType.DMA((parts,)),
        ],
        compiler_params=pltpu.CompilerParams(vmem_limit_bytes=62 << 20),
        cost_estimate=cost(40 * rows * channels, 10 * rows * channels),
        name="product",
    )(taps, branches, filt)


def unrolled(blocks):
    return 4 if blocks <= 8 else 1


def chunk_of(index, offset=0):
    return pl.ds(pl.multiple_of(offset + index * ROWS, ROWS), ROWS)


def column(twist, rows, index, width):
    return jnp.broadcast_to(twist[rows, index : index + 1], (ROWS, width))


def first_rows(signals, taps, length):
    edge = taps.shape[1] - 1
    rims = signals[:, 2 * length :, :].astype(F32)
    result = []
    for branch in range(BRANCHES):
        before, after = (
            [rims[:, (side * BRANCHES + branch) * edge + i, :] for i in range(edge)]
            for side in (0, 1)
        )
        zero = jnp.zeros_like(before[0][:1])
        rows = [jnp.concatenate([zero, row[:-1]], axis=0) for row in before] + after
        smooth = []
        for i in range(edge):
            total = None
            for tap in range(edge + 1):
                term = rows[edge + i - tap] * taps[branch, tap : tap + 1, :]
                total = term if total is None else total + term
            smooth.append(total)
        result.append(smooth)
    return result


def replaced(tile, rows):
    ids = lax.broadcasted_iota(jnp.int32, tile.shape, 0)
    for i, row in enumerate(rows):
        tile = jnp.where(ids == i, jnp.broadcast_to(row, tile.shape), tile)
    return tile


def transform_kernel(matrix, twist, taps, signals, turned, product, gates, waves):
    blocks, length, width = product.shape
    pairs = blocks // 2

    smooth = first_rows(signals, taps, length)
    for b in range(blocks):
        product[b, ROWS:, :] = signals[b, ROWS:length, :]
        heads = [smooth[0][i][b : b + 1] * smooth[2][i][b : b + 1] for i in range(len(smooth[0]))]
        product[b, :ROWS, :] = replaced(signals[b, :ROWS, :].astype(F32), heads).astype(BF16)
        gains = [smooth[1][i][b : b + 1] for i in range(len(smooth[1]))]
        gates[b] = replaced(jnp.ones((ROWS, width), F32), gains)

    def forward(index, carry):
        rows, low = chunk_of(index), chunk_of(index, length)
        turns = [
            (column(twist, rows, k, width), column(twist, rows, blocks + k, width))
            for k in range(blocks)
        ]
        for side in (0, 1):
            lanes = slice(side * width, (side + 1) * width)
            if side == 0:
                values = [product[b, rows, :].astype(F32) for b in range(blocks)]
            else:
                values = [signals[b, low, :].astype(F32) for b in range(blocks)]
            spectra = across_blocks(values)
            waves[0, rows, lanes] = spectra[0][0].astype(BF16)
            for k in range(1, blocks + 1):
                real, imag = spectra[k]
                cosine, sine = turns[k - 1]
                if imag is None:
                    waves[k, rows, lanes] = (real * cosine).astype(BF16)
                    waves[k, low, lanes] = (-real * sine).astype(BF16)
                else:
                    waves[k, rows, lanes] = (real * cosine + imag * sine).astype(BF16)
                    waves[k, low, lanes] = (imag * cosine - real * sine).astype(BF16)
        return carry

    lax.fori_loop(0, length // ROWS, forward, 0, unroll=unrolled(blocks))

    def multiplied(spectrum):
        real, imag = spectrum[:length], spectrum[length:]
        a_real, a_imag = real[:, :width], imag[:, :width]
        b_real, b_imag = real[:, width:], imag[:, width:]
        return jnp.concatenate(
            [
                (a_real * b_real - a_imag * b_imag).astype(BF16),
                (-(a_real * b_imag + a_imag * b_real)).astype(BF16),
            ],
            axis=0,
        )

    def dot(left, right):
        return jnp.dot(left, right, preferred_element_type=F32)

    base = multiplied(dot(matrix[:, :length], waves[0, :length, :]))
    turned[pairs, :length, :width] = dot(matrix[:length, :], base)

    def one_pair(pair):
        left = multiplied(dot(matrix[...], waves[2 * pair + 1]))
        right = multiplied(dot(matrix[...], waves[2 * pair + 2]))
        turned[pair] = dot(matrix[...], jnp.concatenate([left, right], axis=1))

    if pairs <= 4:
        for pair in range(pairs):
            one_pair(pair)
    else:
        lax.fori_loop(0, pairs, lambda pair, carry: (one_pair(pair), carry)[1], 0)


def back_kernel(twist, gain, gates, turned, product, *outs):
    blocks, length, width = product.shape
    full, pairs = 2 * blocks * length, blocks // 2
    skip = jnp.broadcast_to(gain[...], (ROWS, width))

    def backward(out, start, index, carry):
        rows, low = chunk_of(index, start), chunk_of(index, length + start)
        parts = []
        for k in range(1, blocks + 1):
            pair, side = (k - 1) // 2, (k - 1) % 2
            lanes = slice(side * width, (side + 1) * width)
            real, minus = turned[pair, rows, lanes], turned[pair, low, lanes]
            cosine = column(twist, rows, 2 * blocks + k - 1, width)
            sine = column(twist, rows, 3 * blocks + k - 1, width)
            turned_real = real * cosine + minus * sine
            parts.append((turned_real, None if k == blocks else real * sine - minus * cosine))
        first = turned[pairs, rows, :width] * np.float32(1.0 / full)
        for b, value in enumerate(back_to_blocks(first, parts)):
            direct = skip * product[b, rows, :].astype(F32)
            out[b, chunk_of(index), :] = (value + direct).astype(BF16)
        return carry

    start = 0
    for out in outs:
        body = functools.partial(backward, out, start)
        lax.fori_loop(0, out.shape[1] // ROWS, body, 0, unroll=unrolled(blocks))
        start += out.shape[1]
    for b in range(blocks):
        outs[0][b, :ROWS, :] = (outs[0][b, :ROWS, :].astype(F32) * gates[b]).astype(BF16)


def weight_copies(weight, held, sems, block):
    depth, columns = held.shape
    span = pl.ds(pl.multiple_of(block * columns, columns), columns)
    step = depth // PIECES
    pieces = [pl.ds(i * step, step) for i in range(PIECES)]
    return [
        pltpu.make_async_copy(weight.at[rows, span], held.at[rows, :], sems.at[i])
        for i, rows in enumerate(pieces)
    ]


def start_all(copies):
    for copy in copies:
        copy.start()


def project_into(outs, gated, weight, copies, total):
    depth, columns = weight.shape
    group = PIECES // STEPS
    for step in range(STEPS):
        for copy in copies[step * group : (step + 1) * group]:
            copy.wait()
        rows = slice(step * depth // STEPS, (step + 1) * depth // STEPS)
        for start in range(0, columns, TILE):
            span = slice(start, start + TILE)
            value = jnp.dot(gated[:, rows], weight[rows, span], preferred_element_type=F32)
            if step:
                value = total[:, span] + value
            if step < STEPS - 1:
                total[:, span] = value
            else:
                index, offset = divmod(start, columns // len(outs))
                out = outs[index]
                out[:, offset : offset + TILE] = value.astype(out.dtype)


def gated_rows(start, mixed, branch, taps, gated, padded):
    parts, rows, width = mixed.shape
    for j in range(parts):
        lanes = slice(j * width, (j + 1) * width)
        strips = smoothed(branch, lanes, tap_rows(taps, 1, lanes), padded.at[j % 2], rows, start)
        for span, second in strips:
            value = mixed[j, span, :].astype(F32)
            done = second * value
            if start == 0 and span.start == 0:
                ids = lax.broadcasted_iota(jnp.int32, done.shape, 0)
                done = jnp.where(ids < taps.shape[1] - 1, value, done)
            gated[span, lanes] = done.astype(BF16)


def gate_kernel(start, place, mixed, branch, taps, weight, gated, part, padded, held, sems, total):
    copies = weight_copies(weight, held.at[0], sems.at[0], place[0] ^ 3)
    start_all(copies)
    gated_rows(start, mixed, branch, taps, gated, padded)
    project_into([part], gated, held.at[0], copies, total)


def own_kernel(place, gated, weight, own, held, sems, total):
    copies = weight_copies(weight, held.at[0], sems.at[0], place[0] ^ 2)
    start_all(copies)
    project_into([own], gated, held.at[0], copies, total)


def near_kernel(place, first, second, weight, *rest):
    *parts, own, held, sems, total, gated = rest
    sets = [weight_copies(weight, held.at[i], sems.at[i], place[0] ^ (1 - i)) for i in (0, 1)]
    start_all(sets[0])
    start_all(sets[1])
    rows = first.shape[0]
    gated[:rows, :] = first[...]
    gated[rows:, :] = second[...]
    project_into(parts, gated, held.at[0], sets[0], total)
    project_into([own], gated, held.at[1], sets[1], total)


def shards(branches, short_filter, long_filter, skip_gain, out_weight):
    seq_count, mp_count = lax.axis_size("seq"), lax.axis_size("mp")
    tokens, channels = long_filter.shape
    width = channels // seq_count
    features = out_weight.shape[1] // mp_count
    me, place = lax.axis_index("mp").reshape(1), lax.axis_index("seq")
    params = pltpu.CompilerParams(vmem_limit_bytes=50 << 20)
    small = pltpu.CompilerParams(vmem_limit_bytes=24 << 20)

    def exchanged(value, bit):
        return lax.ppermute(value, "mp", [(m, m ^ bit) for m in range(mp_count)])

    def across(value):
        return lax.all_to_all(value, "seq", 0, 0, tiled=True)

    def shape(dtype, rows):
        return jax.ShapeDtypeStruct((rows, features), dtype)

    taps = jnp.transpose(short_filter, (0, 2, 1))
    signals = across(signals_of(branches, taps, long_filter, seq_count))

    mine = place * width
    gain = lax.dynamic_slice(skip_gain, (mine,), (width,)).reshape(1, width)
    my_taps = lax.dynamic_slice_in_dim(taps, mine, width, 2)
    matrix, twist = (jnp.asarray(t) for t in transform_tables(tokens, 2 * seq_count))
    turned, product, gates = pl.pallas_call(
        transform_kernel,
        in_specs=[VMEM] * 4,
        out_specs=[VMEM] * 3,
        out_shape=[
            jax.ShapeDtypeStruct((seq_count // 2 + 1, 2 * tokens, 2 * width), F32),
            jax.ShapeDtypeStruct((seq_count, tokens, width), BF16),
            jax.ShapeDtypeStruct((seq_count, ROWS, width), F32),
        ],
        scratch_shapes=[pltpu.VMEM((seq_count + 1, 2 * tokens, 2 * width), BF16)],
        compiler_params=small,
        cost_estimate=cost(seq_count * 12 * (2 * tokens) ** 2 * width, 6 << 20),
        name="transform",
    )(matrix, twist, my_taps, signals)
    counts = (tokens * 176 // 256, tokens * 80 // 256)
    mixed = pl.pallas_call(
        back_kernel,
        in_specs=[VMEM] * 5,
        out_specs=[VMEM] * len(counts),
        out_shape=[jax.ShapeDtypeStruct((seq_count, count, width), BF16) for count in counts],
        compiler_params=small,
        cost_estimate=cost(200 * tokens * channels, 5 << 20),
        name="back",
    )(twist, gain, gates, turned, product)

    flops, moved = 2 * tokens * channels * features, 2 * channels * features
    held = pltpu.VMEM((2, channels, features), BF16)
    sems = pltpu.SemaphoreType.DMA((2, PIECES))
    gated, far = [], []
    start = 0
    for step, (value, count) in enumerate(zip(mixed, counts)):
        padded = pltpu.VMEM((2, count + ROWS, width), F32)
        total = pltpu.VMEM((count, features), F32)
        if step:
            value, sent = lax.optimization_barrier((value, sent))
        value = across(value)
        ready, part = pl.pallas_call(
            functools.partial(gate_kernel, start),
            in_specs=[SMEM] + [VMEM] * 3 + [HBM],
            out_specs=[VMEM] * 2,
            out_shape=[jax.ShapeDtypeStruct((count, channels), BF16), shape(BF16, count)],
            scratch_shapes=[padded, held, sems, total],
            compiler_params=params,
            cost_estimate=cost(1, 1),
            name="gate",
        )(me, value, branches[1], taps, out_weight)
        other = exchanged(part, 1)
        own = pl.pallas_call(
            own_kernel,
            in_specs=[SMEM, VMEM, HBM],
            out_specs=VMEM,
            out_shape=shape(F32, count),
            scratch_shapes=[held, sems, total],
            compiler_params=params,
            cost_estimate=cost(1, 1),
            name="own",
        )(me, ready, out_weight)
        if step:
            own, far[0] = lax.optimization_barrier((own, far[0]))
        sent = (own + other.astype(F32)).astype(BF16)
        gated.append(ready)
        far.append(exchanged(sent, 2))
        start += count
    gated[0], gated[1], sent = lax.optimization_barrier((gated[0], gated[1], sent))
    pieces = 4
    *near_part, near_own = pl.pallas_call(
        near_kernel,
        in_specs=[SMEM, VMEM, VMEM, HBM],
        out_specs=[VMEM] * (pieces + 1),
        out_shape=[jax.ShapeDtypeStruct((tokens, features // pieces), BF16)] * pieces
        + [shape(F32, tokens)],
        scratch_shapes=[
            held,
            sems,
            pltpu.VMEM((tokens, features), F32),
            pltpu.VMEM((tokens, channels), BF16),
        ],
        compiler_params=params,
        cost_estimate=cost(1, 1),
        name="near",
    )(me, *gated, out_weight)
    near_part = jnp.concatenate([exchanged(part, 1) for part in near_part], axis=1)
    near = near_own + near_part.astype(F32)
    return (near + jnp.concatenate(far, axis=0).astype(F32)).astype(BF16)


def solution(mesh):
    return jax.shard_map(
        shards,
        mesh=mesh,
        in_specs=(
            P(None, "seq", "mp"),
            P(None, "mp", None),
            P("seq", "mp"),
            P("mp"),
            P("mp", None),
        ),
        out_specs=P("seq", "mp"),
        check_vma=False,
    )
```
